32 devices in a mesh: groups: 2 (over x), shot: 16 (over z, y, core).
Axes of the slice: x: 2, y: 2, z: 4, core: 2. Of those that a mesh axis runs over, the one named last changes fastest.
Arguments:
- spectra: bfloat16 [1024, 2, 64, 512], P(('groups', 'shot')), parts along dimension 0, may hold values from -1.1953125 to 1.1953125
- fold_counts: int32 [1024], P('groups'), parts along dimension 0, may hold values from 1 to 512
- inverse_wavelet: float32 [2, 64], replicated, may hold values from -4 to 4
Outputs:
- multiples: bfloat16 [1024, 2, 64, 512], P(('groups', 'shot')), parts along dimension 0
The draws below stay inside these ranges and needn't reach their ends.
There are 2 independent parts, one for each index of `groups`. The reference program is written for one: setup_inputs(seed, part) draws one part's arguments, and reference() takes and returns one part's arrays. A program takes and returns all parts, laid end to end along the dimension named above; an argument that names none is the same for every part. Nothing has to cross between parts.
All inputs are finite; a program needn't handle non-finite values.
Results may differ from the reference program's by a relative error of at most 0.001.
Values may be sent and summed in bfloat16 or wider, within the bound.
A program may use at most 64 MiB of HBM per device.

```python
import jax
import jax.numpy as jnp
from jax import lax

POINTS = 512
BINS = 64


def draw_fold_counts(key, part):
    key_choose = jax.random.fold_in(key, 11)
    key_wide = jax.random.fold_in(key, 12)
    key_pick = jax.random.fold_in(key, 13)
    chooser = jax.random.randint(key_choose, (POINTS,), 0, 2)
    wide = jax.random.randint(key_wide, (POINTS,), POINTS // 2 + 1, POINTS + 1)
    folds = jnp.where(chooser == 1, wide, 1)
    picks = jax.random.permutation(key_pick, POINTS)
    positions = jnp.arange(POINTS, dtype=jnp.int32)
    folds = jnp.where(positions == picks[0], POINTS, folds)
    folds = jnp.where(positions == picks[1], 1, folds)
    return folds.astype(jnp.int32)


def levels(stream_key, dims, split, low, high):
    factor_of, own = 1.0, jax.random.fold_in(stream_key, 6)
    for axis_at, parts in split:
        draws = jnp.exp(jax.random.uniform(jax.random.fold_in(own, axis_at), (parts,), jnp.float32, low / len(split), high / len(split)))
        factor_of = factor_of * jnp.repeat(draws, dims[axis_at] // parts).reshape([-1 if axis == axis_at else 1 for axis in range(len(dims))])
    return factor_of


def bell_draw(stream_key, extent, width, reach, cuts=(), kind=jnp.bfloat16):
    array = width * jax.random.normal(stream_key, extent, jnp.float32)
    if cuts:
        array = array * levels(stream_key, extent, cuts, -0.22, 0.18)
    return jnp.clip(array, -reach, reach).astype(kind)


def setup_inputs(seed: int = 0, part: int = 0) -> dict:
    arg_keys = jax.random.split(jax.random.key(seed), 4)
    part_keys = jax.random.split(jax.random.fold_in(arg_keys[3], part), 4)
    spectra = bell_draw(part_keys[0], (POINTS, 2, BINS, POINTS), 0.2, 1.1953125, ((0, 16),))
    fold_counts = draw_fold_counts(jax.random.fold_in(jax.random.fold_in(arg_keys[3], part), 71), part)
    inverse_wavelet = bell_draw(arg_keys[2], (2, BINS), 1.0, 4.0, (), jnp.float32)
    return dict(spectra=spectra, fold_counts=fold_counts, inverse_wavelet=inverse_wavelet)


def reference(spectra, fold_counts, inverse_wavelet):
    indices = jnp.arange(POINTS, dtype=jnp.int32)
    recorded = jnp.abs(indices[None, :] - indices[:, None]) < fold_counts[:, None]
    mirrored = spectra.transpose(3, 1, 2, 0)
    filled = jnp.where(recorded[:, None, None, :], spectra,
                       jnp.where(recorded.T[:, None, None, :], mirrored, jnp.zeros_like(spectra)))

    def per_bin(which):
        slab = lax.dynamic_index_in_dim(filled, which, 2, keepdims=False)
        real_component = slab[:, 0, :]
        imaginary_component = slab[:, 1, :]
        prod_real = jnp.dot(real_component, real_component, preferred_element_type=jnp.float32) - jnp.dot(imaginary_component, imaginary_component, preferred_element_type=jnp.float32)
        prod_imag = jnp.dot(real_component, imaginary_component, preferred_element_type=jnp.float32) + jnp.dot(imaginary_component, real_component, preferred_element_type=jnp.float32)
        wave = lax.dynamic_index_in_dim(inverse_wavelet, which, 1, keepdims=False)
        output_real = -(wave[0] * prod_real - wave[1] * prod_imag)
        out_imag = -(wave[0] * prod_imag + wave[1] * prod_real)
        return jnp.stack([output_real, out_imag], axis=1).astype(jnp.bfloat16)

    stacked_spectra = lax.map(per_bin, jnp.arange(BINS, dtype=jnp.int32))
    return stacked_spectra.transpose(1, 2, 0, 3)
```

```python
import functools

import jax
import jax.numpy as jnp
from jax import lax
from jax.experimental import pallas as pl
from jax.experimental.pallas import tpu as pltpu
from jax.sharding import PartitionSpec as P

MESH = pl.DeviceIdType.MESH
VMEM_BYTES = 54 * 1024 * 1024
ROWS = 8
LANES = 128


def turn(eye, block):
    return lax.dot_general(eye, block, (((1,), (1,)), ((), ())),
                           preferred_element_type=jnp.float32).astype(jnp.bfloat16)


def kernel(planes, n, x_ref, row_ref, wave_ref, o_ref,
           recv, stage, filled, ostage, out, keep, swap, eye,
           near_column, near_core, near_chip,
           own_in, in_send, column_in, chip_in, core_in, own_out, out_send, out_recv):
    shots, _, _, _, points = x_ref.shape
    tiles = recv.shape[0]
    group = n // planes
    chips = group // 2
    me = lax.axis_index("shot")
    plane, place = me // group, lax.rem(me, group)
    chip, core = place // 2, lax.rem(place, 2)
    sibling = me + 1 - 2 * core

    def in_column(q):
        return q * group + place

    def in_plane(k):
        return plane * group + 2 * k + core

    def signal(sem, to):
        pl.semaphore_signal(sem, inc=1, device_id={"shot": to}, device_id_type=MESH)

    barrier = pltpu.get_barrier_semaphore()
    for q in range(planes):
        pl.when(q > plane)(lambda q=q: signal(barrier, in_column(q)))
    pl.when(core == 0)(lambda: signal(barrier, sibling))
    for k in range(chips):
        pl.when(k > chip)(lambda k=k: signal(barrier, in_plane(k)))
    lower = plane + core + chip
    pl.when(lower > 0)(lambda: pl.semaphore_wait(barrier, lower))
    for q in range(planes):
        pl.when(q < plane)(lambda q=q: signal(near_column.at[plane], in_column(q)))
    pl.when(core == 1)(lambda: signal(near_core, sibling))
    for k in range(chips):
        pl.when(k < chip)(lambda k=k: signal(near_chip.at[chip], in_plane(k)))

    def send(src, t, source, sem, to):
        pltpu.make_async_remote_copy(src, recv.at[t, source], in_send, sem,
                                     device_id={"shot": to}, device_id_type=MESH).start()

    def own(q, t):
        return x_ref.at[:, :, q * tiles + t]

    for t in range(tiles):
        for q in range(planes):
            pl.when(q < plane)(lambda q=q: send(own(q, t), t, me, column_in.at[t, plane], in_column(q)))
        if t == 0:
            pl.when(core == 0)(lambda: pl.semaphore_wait(near_core, 1))
        send(own(plane, t), t, me, core_in.at[t], sibling)
        for k in range(chips):
            if t == 0:
                pl.when(k > chip)(lambda k=k: pl.semaphore_wait(near_chip.at[k], 1))
            pl.when(k != chip)(lambda k=k: send(own(plane, t), t, me, chip_in.at[t, plane, chip], in_plane(k)))
        for q in range(planes):
            if t == 0:
                pl.when(q > plane)(lambda q=q: pl.semaphore_wait(near_column.at[q], 1))
            pl.when(q > plane)(lambda q=q: send(own(q, t), t, me, column_in.at[t, plane], in_column(q)))
        pltpu.make_async_copy(own(plane, t), recv.at[t, me], own_in.at[t]).start()

    shot = lax.broadcasted_iota(jnp.int32, (points, points), 0)
    point = lax.broadcasted_iota(jnp.int32, (points, points), 1)
    eye[...] = jnp.where(shot == point, 1.0, 0.0).astype(jnp.bfloat16)
    mirrored = jnp.where(jnp.abs(shot - point) < row_ref[...], 1.0, 0.0).astype(jnp.bfloat16)
    keep[...] = turn(eye[...], mirrored)
    swap[...] = keep[...] * (1.0 - mirrored)

    def landed(t, source, sem):
        pltpu.make_async_copy(recv.at[t, source], recv.at[t, source], sem).wait()

    def pass_on(t):
        def from_chips(q):
            for k in range(chips):
                @pl.when(k != chip)
                def _(k=k):
                    source = q * group + 2 * k + core
                    landed(t, source, chip_in.at[t, q, k])
                    send(recv.at[t, source], t, source, core_in.at[t], sibling)

        def from_plane(q):
            source = in_column(q)
            landed(t, source, column_in.at[t, q])
            for k in range(chips):
                pl.when(k != chip)(
                    lambda k=k: send(recv.at[t, source], t, source, chip_in.at[t, q, chip], in_plane(k)))
            send(recv.at[t, source], t, source, core_in.at[t], sibling)

        @pl.loop(1, planes)
        def _(d):
            pl.when(plane - d >= 0)(lambda: from_plane(plane - d))
            pl.when(plane + d < planes)(lambda: from_plane(plane + d))

        from_chips(plane)

        @pl.loop(1, planes)
        def _(d):
            pl.when(plane - d >= 0)(lambda: from_chips(plane - d))
            pl.when(plane + d < planes)(lambda: from_chips(plane + d))

        landed(t, me, own_in.at[t])
        half = pl.ds(0, n // 2)
        pltpu.make_async_copy(recv.at[t, half], recv.at[t, half], core_in.at[t]).wait()

    few = 8

    def fill(t, c):
        @pl.loop(0, points // few)
        def _(i):
            source = (i * few) // shots
            rows = recv[t, source, pl.ds(lax.rem(i * few, shots), few), c].astype(jnp.float32)
            rows = rows.reshape(few * ROWS, points)
            for q in range(points // LANES):
                stage[q, pl.ds(pl.multiple_of(i * few * ROWS, few * ROWS), few * ROWS), :] = (
                    rows[:, q * LANES : (q + 1) * LANES])

        @pl.loop(0, ROWS)
        def _(f):
            for q in range(points // LANES):
                filled[f, c, :, pl.ds(q * LANES, LANES)] = (
                    stage[q, pl.ds(f, points, stride=ROWS), :].astype(jnp.bfloat16))
            block = filled[f, c]
            filled[f, c] = block * keep[...] + turn(eye[...], block * swap[...])

    def multiply(t):
        height = planes * shots

        @pl.loop(0, ROWS)
        def _(f):
            left = jnp.concatenate(
                [filled[f, c, pl.ds(pl.multiple_of(in_column(q) * shots, shots), shots), :]
                 for c in range(2) for q in range(planes)], axis=0)
            dot = functools.partial(jnp.dot, preferred_element_type=jnp.float32)
            by_real, by_imag = dot(left, filled[f, 0]), dot(left, filled[f, 1])
            prod_real = by_real[:height] - by_imag[height:]
            prod_imag = by_imag[:height] + by_real[height:]
            which = (plane * tiles + t) * ROWS + f
            wave_real, wave_imag = wave_ref[0, which], wave_ref[1, which]
            out_real = -(wave_real * prod_real - wave_imag * prod_imag)
            out_imag = -(wave_real * prod_imag + wave_imag * prod_real)
            for q in range(points // LANES):
                lanes = slice(q * LANES, (q + 1) * LANES)
                ostage[0, q, pl.ds(f, height, stride=ROWS), :] = out_real[:, lanes]
                ostage[1, q, pl.ds(f, height, stride=ROWS), :] = out_imag[:, lanes]

        @pl.loop(0, planes)
        def _(z):
            rows = pl.ds(pl.multiple_of(z * shots * ROWS, shots * ROWS), shots * ROWS)
            for c in range(2):
                for q in range(points // LANES):
                    block = ostage[c, q, rows, :].reshape(shots, ROWS, LANES)
                    out[t, z, :, c, :, pl.ds(q * LANES, LANES)] = block.astype(jnp.bfloat16)

    @pl.loop(0, tiles)
    def _(t):
        pass_on(t)

        @pl.loop(0, 2)
        def _(c):
            fill(t, c)

        multiply(t)
        theirs = o_ref.at[:, :, plane * tiles + t]
        for q in range(planes):
            @pl.when(q != plane)
            def _(q=q):
                pltpu.make_async_remote_copy(out.at[t, q], theirs, out_send, out_recv,
                                             device_id={"shot": in_column(q)}, device_id_type=MESH).start()
        pltpu.make_async_copy(out.at[t, plane], theirs, own_out.at[t]).start()

    for t in range(tiles):
        pltpu.make_async_copy(out.at[t, 0], o_ref.at[:, :, t], own_out.at[t]).wait()
    sent = recv.at[:, pl.ds(0, n - 1)]
    pltpu.make_async_copy(sent, sent, in_send).wait()
    others = o_ref.at[:, :, pl.ds(0, (planes - 1) * tiles)]
    pltpu.make_async_copy(others, others, out_send).wait()
    pltpu.make_async_copy(others, others, out_recv).wait()


def shards(n, spectra, fold_counts, inverse_wavelet):
    shots, _, bins, points = spectra.shape
    bf16, f32 = jnp.bfloat16, jnp.float32
    tiles = 2
    planes = bins // (tiles * ROWS)
    tiled = (shots, 2, bins // ROWS, ROWS, points)
    height = planes * shots
    landed = pl.pallas_call(
        functools.partial(kernel, planes, n),
        out_shape=pltpu.VMEM(tiled, bf16),
        in_specs=[pl.BlockSpec(memory_space=pl.ANY), pl.BlockSpec(memory_space=pltpu.VMEM),
                  pl.BlockSpec(memory_space=pltpu.SMEM)],
        out_specs=pl.BlockSpec(memory_space=pltpu.VMEM),
        scratch_shapes=[
            pltpu.VMEM((tiles, n, shots, 2, ROWS, points), bf16),
            pltpu.VMEM((points // LANES, points * ROWS, LANES), f32),
            pltpu.VMEM((ROWS, 2, points, points), bf16),
            pltpu.VMEM((2, points // LANES, height * ROWS, LANES), f32),
            pltpu.VMEM((tiles, planes, shots, 2, ROWS, points), bf16),
            pltpu.VMEM((points, points), bf16),
            pltpu.VMEM((points, points), bf16),
            pltpu.VMEM((points, points), bf16),
            pltpu.SemaphoreType.REGULAR((planes,)),
            pltpu.SemaphoreType.REGULAR,
            pltpu.SemaphoreType.REGULAR((n // planes // 2,)),
            pltpu.SemaphoreType.DMA((tiles,)),
            pltpu.SemaphoreType.DMA,
            pltpu.SemaphoreType.DMA((tiles, planes)),
            pltpu.SemaphoreType.DMA((tiles, planes, n // planes // 2)),
            pltpu.SemaphoreType.DMA((tiles,)),
            pltpu.SemaphoreType.DMA((tiles,)),
            pltpu.SemaphoreType.DMA,
            pltpu.SemaphoreType.DMA,
        ],
        compiler_params=pltpu.CompilerParams(
            collective_id=0, has_side_effects=True, vmem_limit_bytes=VMEM_BYTES),
    )(spectra.reshape(tiled), fold_counts[None, :], inverse_wavelet)
    return landed.reshape(spectra.shape)


def solution(mesh):
    spec = P(("groups", "shot"), None, None, None)
    return jax.shard_map(functools.partial(shards, mesh.shape["shot"]), mesh=mesh,
                         in_specs=(spec, P("groups"), P()), out_specs=spec, check_vma=False)
```

```python
import functools

import jax
import jax.numpy as jnp
from jax import lax
from jax.experimental import pallas as pl
from jax.experimental.pallas import tpu as pltpu
from jax.sharding import PartitionSpec as P

MESH = pl.DeviceIdType.MESH
VMEM_BYTES = 50 * 1024 * 1024
ROWS = 8
LANES = 128


def turn(eye, block):
    return lax.dot_general(eye, block, (((1,), (1,)), ((), ())),
                           preferred_element_type=jnp.float32).astype(jnp.bfloat16)


def kernel(planes, n, x_ref, row_ref, wave_ref, o_ref,
           land, stage, traces, filled, ostage, out, keep, swap, eye,
           near_column, near_core, near_chip,
           own_in, in_send, column_in, chip_in, core_in, own_out, out_send, out_recv):
    shots, _, _, _, points = x_ref.shape
    tiles = land.shape[0]
    group = n // planes
    chips = group // 2
    me = lax.axis_index("shot")
    plane, place = me // group, lax.rem(me, group)
    chip, core = place // 2, lax.rem(place, 2)
    sibling = me + 1 - 2 * core

    def in_column(q):
        return q * group + place

    def in_plane(k):
        return plane * group + 2 * k + core

    def signal(sem, to):
        pl.semaphore_signal(sem, inc=1, device_id={"shot": to}, device_id_type=MESH)

    barrier = pltpu.get_barrier_semaphore()
    for q in range(planes):
        pl.when(q > plane)(lambda q=q: signal(barrier, in_column(q)))
    pl.when(core == 0)(lambda: signal(barrier, sibling))
    for k in range(chips):
        pl.when(k > chip)(lambda k=k: signal(barrier, in_plane(k)))
    lower = plane + core + chip
    pl.when(lower > 0)(lambda: pl.semaphore_wait(barrier, lower))
    for q in range(planes):
        pl.when(q < plane)(lambda q=q: signal(near_column.at[plane], in_column(q)))
    pl.when(core == 1)(lambda: signal(near_core, sibling))
    for k in range(chips):
        pl.when(k < chip)(lambda k=k: signal(near_chip.at[chip], in_plane(k)))

    def rows_of(source):
        return pl.ds(pl.multiple_of(source * shots, shots), shots)

    def send(src, dst, sem, to):
        pltpu.make_async_remote_copy(src, dst, in_send, sem, device_id={"shot": to}, device_id_type=MESH).start()

    def own(q, t):
        return x_ref.at[:, :, q * tiles + t]

    for t in range(tiles):
        pltpu.make_async_copy(own(plane, t), land.at[t, plane], own_in.at[t]).start()

    def send_traces(q, t):
        send(own(q, t), land.at[t, plane], column_in.at[t, plane], in_column(q))

    for t in range(tiles):
        for q in range(planes):
            pl.when(q < plane)(lambda q=q: send_traces(q, t))
        for q in range(planes):
            if t == 0:
                pl.when(q > plane)(lambda q=q: pl.semaphore_wait(near_column.at[q], 1))
            pl.when(q > plane)(lambda q=q: send_traces(q, t))

    def share(t, q):
        for c in range(2):
            flat = land[t, q, :, c].astype(jnp.float32).reshape(shots * ROWS, points)
            for k in range(points // LANES):
                stage[c, k] = flat[:, k * LANES : (k + 1) * LANES]
        mine = rows_of(in_column(q))
        for c in range(2):
            for f in range(ROWS):
                for k in range(points // LANES):
                    traces[t, f, c, mine, pl.ds(k * LANES, LANES)] = (
                        stage[c, k, pl.ds(f, shots, stride=ROWS), :].astype(jnp.bfloat16))
        piece = traces.at[t, :, :, mine]
        for k in range(chips):
            pl.when(k != chip)(lambda k=k: send(piece, piece, chip_in.at[t, q, chip], in_plane(k)))
        send(piece, piece, core_in.at[t], sibling)

    pl.when(core == 0)(lambda: pl.semaphore_wait(near_core, 1))
    for k in range(chips):
        pl.when(k > chip)(lambda k=k: pl.semaphore_wait(near_chip.at[k], 1))

    @pl.loop(0, tiles)
    def _(t):
        pltpu.make_async_copy(land.at[t, plane], land.at[t, plane], own_in.at[t]).wait()
        share(t, plane)

    shot = lax.broadcasted_iota(jnp.int32, (points, points), 0)
    point = lax.broadcasted_iota(jnp.int32, (points, points), 1)
    eye[...] = jnp.where(shot == point, 1.0, 0.0).astype(jnp.bfloat16)
    mirrored = jnp.where(jnp.abs(shot - point) < row_ref[...], 1.0, 0.0).astype(jnp.bfloat16)
    keep[...] = turn(eye[...], mirrored)
    swap[...] = keep[...] * (1.0 - mirrored)

    def nearest_first(work):
        @pl.loop(1, planes)
        def _(d):
            pl.when(plane - d >= 0)(lambda: work(plane - d))
            pl.when(plane + d < planes)(lambda: work(plane + d))

    def from_columns(t):
        def one(q):
            pltpu.make_async_copy(land.at[t, q], land.at[t, q], column_in.at[t, q]).wait()
            share(t, q)

        nearest_first(one)

    def from_chips(t):
        def one(q):
            for k in range(chips):
                @pl.when(k != chip)
                def _(k=k):
                    piece = traces.at[t, :, :, rows_of(q * group + 2 * k + core)]
                    pltpu.make_async_copy(piece, piece, chip_in.at[t, q, k]).wait()
                    send(piece, piece, core_in.at[t], sibling)

        one(plane)
        nearest_first(one)
        half = traces.at[t, :, :, pl.ds(0, n // 2 * shots)]
        pltpu.make_async_copy(half, half, core_in.at[t]).wait()

    def fill(t):
        @pl.loop(0, ROWS)
        def _(f):
            for c in range(2):
                block = traces[t, f, c]
                filled[f, c] = block * keep[...] + turn(eye[...], block * swap[...])

    def multiply(t):
        height = planes * shots

        @pl.loop(0, ROWS)
        def _(f):
            left = jnp.concatenate(
                [filled[f, c, pl.ds(pl.multiple_of(in_column(q) * shots, shots), shots), :]
                 for c in range(2) for q in range(planes)], axis=0)
            dot = functools.partial(jnp.dot, preferred_element_type=jnp.float32)
            by_real, by_imag = dot(left, filled[f, 0]), dot(left, filled[f, 1])
            prod_real = by_real[:height] - by_imag[height:]
            prod_imag = by_imag[:height] + by_real[height:]
            which = (plane * tiles + t) * ROWS + f
            wave_real, wave_imag = wave_ref[0, which], wave_ref[1, which]
            out_real = -(wave_real * prod_real - wave_imag * prod_imag)
            out_imag = -(wave_real * prod_imag + wave_imag * prod_real)
            for q in range(points // LANES):
                lanes = slice(q * LANES, (q + 1) * LANES)
                ostage[0, q, pl.ds(f, height, stride=ROWS), :] = out_real[:, lanes]
                ostage[1, q, pl.ds(f, height, stride=ROWS), :] = out_imag[:, lanes]

        @pl.loop(0, planes)
        def _(z):
            rows = pl.ds(pl.multiple_of(z * shots * ROWS, shots * ROWS), shots * ROWS)
            for c in range(2):
                for q in range(points // LANES):
                    block = ostage[c, q, rows, :].reshape(shots, ROWS, LANES)
                    out[t, z, :, c, :, pl.ds(q * LANES, LANES)] = block.astype(jnp.bfloat16)

    def send_results(t):
        theirs = o_ref.at[:, :, plane * tiles + t]
        for q in range(planes):
            @pl.when(q != plane)
            def _(q=q):
                pltpu.make_async_remote_copy(out.at[t, q], theirs, out_send, out_recv,
                                             device_id={"shot": in_column(q)}, device_id_type=MESH).start()
        pltpu.make_async_copy(out.at[t, plane], theirs, own_out.at[t]).start()

    @pl.loop(0, tiles)
    def _(t):
        from_columns(t)
        pl.when(t > 0)(lambda: send_results(t - 1))
        from_chips(t)
        fill(t)
        multiply(t)

    send_results(tiles - 1)
    for t in range(tiles):
        pltpu.make_async_copy(out.at[t, 0], o_ref.at[:, :, t], own_out.at[t]).wait()
    sent = traces.at[:, :, :, pl.ds(0, (n - 1) * shots)]
    pltpu.make_async_copy(sent, sent, in_send).wait()
    others = o_ref.at[:, :, pl.ds(0, (planes - 1) * tiles)]
    pltpu.make_async_copy(others, others, out_send).wait()
    pltpu.make_async_copy(others, others, out_recv).wait()


def shards(n, spectra, fold_counts, inverse_wavelet):
    shots, _, bins, points = spectra.shape
    bf16, f32 = jnp.bfloat16, jnp.float32
    tiles = 2
    planes = bins // (tiles * ROWS)
    tiled = (shots, 2, bins // ROWS, ROWS, points)
    height = planes * shots
    landed = pl.pallas_call(
        functools.partial(kernel, planes, n),
        out_shape=pltpu.VMEM(tiled, bf16),
        in_specs=[pl.BlockSpec(memory_space=pl.ANY), pl.BlockSpec(memory_space=pltpu.VMEM),
                  pl.BlockSpec(memory_space=pltpu.SMEM)],
        out_specs=pl.BlockSpec(memory_space=pltpu.VMEM),
        scratch_shapes=[
            pltpu.VMEM((tiles, planes, shots, 2, ROWS, points), bf16),
            pltpu.VMEM((2, points // LANES, shots * ROWS, LANES), f32),
            pltpu.VMEM((tiles, ROWS, 2, points, points), bf16),
            pltpu.VMEM((ROWS, 2, points, points), bf16),
            pltpu.VMEM((2, points // LANES, height * ROWS, LANES), f32),
            pltpu.VMEM((tiles, planes, shots, 2, ROWS, points), bf16),
            pltpu.VMEM((points, points), bf16),
            pltpu.VMEM((points, points), bf16),
            pltpu.VMEM((points, points), bf16),
            pltpu.SemaphoreType.REGULAR((planes,)),
            pltpu.SemaphoreType.REGULAR,
            pltpu.SemaphoreType.REGULAR((n // planes // 2,)),
            pltpu.SemaphoreType.DMA((tiles,)),
            pltpu.SemaphoreType.DMA,
            pltpu.SemaphoreType.DMA((tiles, planes)),
            pltpu.SemaphoreType.DMA((tiles, planes, n // planes // 2)),
            pltpu.SemaphoreType.DMA((tiles,)),
            pltpu.SemaphoreType.DMA((tiles,)),
            pltpu.SemaphoreType.DMA,
            pltpu.SemaphoreType.DMA,
        ],
        compiler_params=pltpu.CompilerParams(
            collective_id=0, has_side_effects=True, vmem_limit_bytes=VMEM_BYTES),
    )(spectra.reshape(tiled), fold_counts[None, :], inverse_wavelet)
    return landed.reshape(spectra.shape)


def solution(mesh):
    spec = P(("groups", "shot"), None, None, None)
    return jax.shard_map(functools.partial(shards, mesh.shape["shot"]), mesh=mesh,
                         in_specs=(spec, P("groups"), P()), out_specs=spec, check_vma=False)
```

```python
import functools

import jax
import jax.numpy as jnp
from jax import lax
from jax.experimental import pallas as pl
from jax.experimental.pallas import tpu as pltpu
from jax.sharding import PartitionSpec as P

MESH = pl.DeviceIdType.MESH
VMEM_BYTES = 50 * 1024 * 1024
ROWS = 8
LANES = 128


def turn(eye, block):
    return lax.dot_general(eye, block, (((1,), (1,)), ((), ())),
                           preferred_element_type=jnp.float32).astype(jnp.bfloat16)


def kernel(planes, n, x_ref, row_hbm, wave_hbm, o_ref,
           land, stage, traces, filled, ostage, out, keep, swap, eye, row_ref, wave_ref,
           near_column, near_core, near_chip, go,
           small_in, own_in, in_send, column_out, column_in, chip_in, core_in, own_out, out_send, out_recv):
    shots, _, _, _, points = x_ref.shape
    tiles = land.shape[0]
    group = n // planes
    chips = group // 2
    me = lax.axis_index("shot")
    plane, place = me // group, lax.rem(me, group)
    chip, core = place // 2, lax.rem(place, 2)
    sibling = me + 1 - 2 * core

    def in_column(q):
        return q * group + place

    def in_plane(k):
        return plane * group + 2 * k + core

    def signal(sem, to):
        pl.semaphore_signal(sem, inc=1, device_id={"shot": to}, device_id_type=MESH)

    barrier = pltpu.get_barrier_semaphore()
    for q in range(planes):
        pl.when(q > plane)(lambda q=q: signal(barrier, in_column(q)))
    pl.when(core == 0)(lambda: signal(barrier, sibling))
    for k in range(chips):
        pl.when(k > chip)(lambda k=k: signal(barrier, in_plane(k)))
    lower = plane + core + chip
    pl.when(lower > 0)(lambda: pl.semaphore_wait(barrier, lower))
    for q in range(planes):
        pl.when(q < plane)(lambda q=q: signal(near_column.at[plane], in_column(q)))
    pl.when(core == 1)(lambda: signal(near_core, sibling))
    for k in range(chips):
        pl.when(k < chip)(lambda k=k: signal(near_chip.at[chip], in_plane(k)))

    def rows_of(source):
        return pl.ds(pl.multiple_of(source * shots, shots), shots)

    def send(src, dst, sem, to):
        pltpu.make_async_remote_copy(src, dst, in_send, sem, device_id={"shot": to}, device_id_type=MESH).start()

    held = (plane < planes // 2 - 1) | (plane > planes // 2)
    outward = jnp.where(plane < planes // 2, plane - 1, plane + 1)

    def own(q, t):
        return x_ref.at[:, :, q * tiles + t]

    def send_traces(q, t):
        pltpu.make_async_remote_copy(own(q, t), land.at[t, plane], column_out.at[t], column_in.at[t, plane],
                                     device_id={"shot": in_column(q)}, device_id_type=MESH).start()

    def send_all_traces(t):
        for q in range(planes):
            pl.when(q != plane)(lambda q=q: send_traces(q, t))

    for q in range(planes):
        pl.when(q < plane)(lambda q=q: send_traces(q, 0))
    for q in range(planes):
        @pl.when(q > plane)
        def _(q=q):
            pl.semaphore_wait(near_column.at[q], 1)
            send_traces(q, 0)

    @pl.when(jnp.logical_not(held))
    def _():
        for t in range(1, tiles):
            send_all_traces(t)

    for t in range(tiles):
        pltpu.make_async_copy(own(plane, t), land.at[t, plane], own_in.at[t]).start()
    small = [pltpu.make_async_copy(row_hbm, row_ref, small_in.at[0]), pltpu.make_async_copy(wave_hbm, wave_ref, small_in.at[1])]
    for copy in small:
        copy.start()

    def share(t, q):
        for c in range(2):
            flat = land[t, q, :, c].astype(jnp.float32).reshape(shots * ROWS, points)
            for k in range(points // LANES):
                stage[c, k] = flat[:, k * LANES : (k + 1) * LANES]
        mine = rows_of(in_column(q))
        for c in range(2):
            for f in range(ROWS):
                for k in range(points // LANES):
                    traces[t, f, c, mine, pl.ds(k * LANES, LANES)] = (
                        stage[c, k, pl.ds(f, shots, stride=ROWS), :].astype(jnp.bfloat16))
        piece = traces.at[t, :, :, mine]
        for k in range(chips):
            pl.when(k != chip)(lambda k=k: send(piece, piece, chip_in.at[t, q, chip], in_plane(k)))
        send(piece, piece, core_in.at[t], sibling)

    pl.when(core == 0)(lambda: pl.semaphore_wait(near_core, 1))
    for k in range(chips):
        pl.when(k > chip)(lambda k=k: pl.semaphore_wait(near_chip.at[k], 1))

    @pl.loop(0, tiles)
    def _(t):
        pltpu.make_async_copy(land.at[t, plane], land.at[t, plane], own_in.at[t]).wait()
        share(t, plane)

    for copy in small:
        copy.wait()
    shot = lax.broadcasted_iota(jnp.int32, (points, points), 0)
    point = lax.broadcasted_iota(jnp.int32, (points, points), 1)
    eye[...] = jnp.where(shot == point, 1.0, 0.0).astype(jnp.bfloat16)
    mirrored = jnp.where(jnp.abs(shot - point) < row_ref[...], 1.0, 0.0).astype(jnp.bfloat16)
    keep[...] = turn(eye[...], mirrored)
    swap[...] = keep[...] * (1.0 - mirrored)

    def nearest_first(work):
        @pl.loop(1, planes)
        def _(d):
            pl.when(plane - d >= 0)(lambda: work(plane - d))
            pl.when(plane + d < planes)(lambda: work(plane + d))

    def from_columns(t):
        def one(q):
            pltpu.make_async_copy(land.at[t, q], land.at[t, q], column_in.at[t, q]).wait()
            share(t, q)

        nearest_first(one)

    def from_chips(t):
        def one(q):
            for k in range(chips):
                @pl.when(k != chip)
                def _(k=k):
                    piece = traces.at[t, :, :, rows_of(q * group + 2 * k + core)]
                    pltpu.make_async_copy(piece, piece, chip_in.at[t, q, k]).wait()
                    send(piece, piece, core_in.at[t], sibling)

        one(plane)
        nearest_first(one)
        half = traces.at[t, :, :, pl.ds(0, n // 2 * shots)]
        pltpu.make_async_copy(half, half, core_in.at[t]).wait()

    def fill(t):
        @pl.loop(0, ROWS)
        def _(f):
            for c in range(2):
                block = traces[t, f, c]
                filled[f, c] = block * keep[...] + turn(eye[...], block * swap[...])

    def multiply(t):
        height = planes * shots

        @pl.loop(0, ROWS)
        def _(f):
            left = jnp.concatenate(
                [filled[f, c, pl.ds(pl.multiple_of(in_column(q) * shots, shots), shots), :]
                 for c in range(2) for q in range(planes)], axis=0)
            dot = functools.partial(jnp.dot, preferred_element_type=jnp.float32)
            by_real, by_imag = dot(left, filled[f, 0]), dot(left, filled[f, 1])
            prod_real = by_real[:height] - by_imag[height:]
            prod_imag = by_imag[:height] + by_real[height:]
            which = (plane * tiles + t) * ROWS + f
            wave_real, wave_imag = wave_ref[0, which], wave_ref[1, which]
            out_real = -(wave_real * prod_real - wave_imag * prod_imag)
            out_imag = -(wave_real * prod_imag + wave_imag * prod_real)
            for q in range(points // LANES):
                lanes = slice(q * LANES, (q + 1) * LANES)
                ostage[0, q, pl.ds(f, height, stride=ROWS), :] = out_real[:, lanes]
                ostage[1, q, pl.ds(f, height, stride=ROWS), :] = out_imag[:, lanes]

        @pl.loop(0, planes)
        def _(z):
            rows = pl.ds(pl.multiple_of(z * shots * ROWS, shots * ROWS), shots * ROWS)
            for c in range(2):
                for q in range(points // LANES):
                    block = ostage[c, q, rows, :].reshape(shots, ROWS, LANES)
                    out[t, z, :, c, :, pl.ds(q * LANES, LANES)] = block.astype(jnp.bfloat16)

    def send_results(t):
        theirs = o_ref.at[:, :, plane * tiles + t]
        for q in range(planes):
            @pl.when(q != plane)
            def _(q=q):
                pltpu.make_async_remote_copy(out.at[t, q], theirs, out_send, out_recv,
                                             device_id={"shot": in_column(q)}, device_id_type=MESH).start()
        pltpu.make_async_copy(out.at[t, plane], theirs, own_out.at[t]).start()

    @pl.loop(0, tiles)
    def _(t):
        from_columns(t)
        sent = land.at[t, pl.ds(0, planes - 1)]
        pltpu.make_async_copy(sent, sent, column_out.at[t]).wait()
        pl.when((plane > 0) & (plane < planes - 1))(lambda: signal(go.at[t], in_column(outward)))

        @pl.when(held)
        def _():
            pl.semaphore_wait(go.at[t], 1)
            pl.when(t > 0)(lambda: send_results(t - 1))
            pl.when(t < tiles - 1)(lambda: send_all_traces(t + 1))

        from_chips(t)
        fill(t)
        multiply(t)
        pl.when((t == tiles - 1) | jnp.logical_not(held))(lambda: send_results(t))

    for t in range(tiles):
        pltpu.make_async_copy(out.at[t, 0], o_ref.at[:, :, t], own_out.at[t]).wait()
    shared = traces.at[:, :, :, pl.ds(0, (n - planes) * shots)]
    pltpu.make_async_copy(shared, shared, in_send).wait()
    others = o_ref.at[:, :, pl.ds(0, (planes - 1) * tiles)]
    pltpu.make_async_copy(others, others, out_send).wait()
    pltpu.make_async_copy(others, others, out_recv).wait()


def shards(n, spectra, fold_counts, inverse_wavelet):
    shots, _, bins, points = spectra.shape
    bf16, f32 = jnp.bfloat16, jnp.float32
    tiles = 2
    planes = bins // (tiles * ROWS)
    tiled = (shots, 2, bins // ROWS, ROWS, points)
    height = planes * shots
    landed = pl.pallas_call(
        functools.partial(kernel, planes, n),
        out_shape=pltpu.VMEM(tiled, bf16),
        in_specs=[pl.BlockSpec(memory_space=pl.ANY)] * 3,
        out_specs=pl.BlockSpec(memory_space=pltpu.VMEM),
        scratch_shapes=[
            pltpu.VMEM((tiles, planes, shots, 2, ROWS, points), bf16),
            pltpu.VMEM((2, points // LANES, shots * ROWS, LANES), f32),
            pltpu.VMEM((tiles, ROWS, 2, points, points), bf16),
            pltpu.VMEM((ROWS, 2, points, points), bf16),
            pltpu.VMEM((2, points // LANES, height * ROWS, LANES), f32),
            pltpu.VMEM((tiles, planes, shots, 2, ROWS, points), bf16),
            pltpu.VMEM((points, points), bf16),
            pltpu.VMEM((points, points), bf16),
            pltpu.VMEM((points, points), bf16),
            pltpu.VMEM((1, points), jnp.int32),
            pltpu.SMEM((2, bins), f32),
            pltpu.SemaphoreType.REGULAR((planes,)),
            pltpu.SemaphoreType.REGULAR,
            pltpu.SemaphoreType.REGULAR((n // planes // 2,)),
            pltpu.SemaphoreType.REGULAR((tiles,)),
            pltpu.SemaphoreType.DMA((2,)),
            pltpu.SemaphoreType.DMA((tiles,)),
            pltpu.SemaphoreType.DMA,
            pltpu.SemaphoreType.DMA((tiles,)),
            pltpu.SemaphoreType.DMA((tiles, planes)),
            pltpu.SemaphoreType.DMA((tiles, planes, n // planes // 2)),
            pltpu.SemaphoreType.DMA((tiles,)),
            pltpu.SemaphoreType.DMA((tiles,)),
            pltpu.SemaphoreType.DMA,
            pltpu.SemaphoreType.DMA,
        ],
        compiler_params=pltpu.CompilerParams(
            collective_id=0, has_side_effects=True, vmem_limit_bytes=VMEM_BYTES),
    )(spectra.reshape(tiled), fold_counts[None, :], inverse_wavelet)
    return landed.reshape(spectra.shape)


def solution(mesh):
    spec = P(("groups", "shot"), None, None, None)
    return jax.shard_map(functools.partial(shards, mesh.shape["shot"]), mesh=mesh,
                         in_specs=(spec, P("groups"), P()), out_specs=spec, check_vma=False)
```

```python
import functools

import jax
import jax.numpy as jnp
from jax import lax
from jax.experimental import pallas as pl
from jax.experimental.pallas import tpu as pltpu
from jax.sharding import PartitionSpec as P

MESH = pl.DeviceIdType.MESH
VMEM_BYTES = 50 * 1024 * 1024
ROWS = 8
LANES = 128


def turn(eye, block):
    return lax.dot_general(eye, block, (((1,), (1,)), ((), ())),
                           preferred_element_type=jnp.float32).astype(jnp.bfloat16)


def kernel(planes, n, x_ref, row_hbm, wave_hbm, o_ref,
           land, stage, traces, filled, ostage, out, keep, swap, eye, row_ref, wave_ref,
           near_column, near_core, near_chip, go,
           first, first_in, small_in, own_in, in_send, column_out, column_in, chip_in, core_in, own_out, out_send, out_recv):
    shots, _, _, _, points = x_ref.shape
    tiles = land.shape[0]
    group = n // planes
    chips = group // 2
    me = lax.axis_index("shot")
    plane, place = me // group, lax.rem(me, group)
    chip, core = place // 2, lax.rem(place, 2)
    sibling = me + 1 - 2 * core

    def in_column(q):
        return q * group + place

    def in_plane(k):
        return plane * group + 2 * k + core

    def signal(sem, to):
        pl.semaphore_signal(sem, inc=1, device_id={"shot": to}, device_id_type=MESH)

    barrier = pltpu.get_barrier_semaphore()
    for q in range(planes):
        pl.when(q > plane)(lambda q=q: signal(barrier, in_column(q)))
    pl.when(core == 0)(lambda: signal(barrier, sibling))
    for k in range(chips):
        pl.when(k > chip)(lambda k=k: signal(barrier, in_plane(k)))
    lower = plane + core + chip
    pl.when(lower > 0)(lambda: pl.semaphore_wait(barrier, lower))
    for q in range(planes):
        pl.when(q < plane)(lambda q=q: signal(near_column.at[plane], in_column(q)))
    pl.when(core == 1)(lambda: signal(near_core, sibling))
    for k in range(chips):
        pl.when(k < chip)(lambda k=k: signal(near_chip.at[chip], in_plane(k)))

    def rows_of(source):
        return pl.ds(pl.multiple_of(source * shots, shots), shots)

    def send(src, dst, sem, to):
        pltpu.make_async_remote_copy(src, dst, in_send, sem, device_id={"shot": to}, device_id_type=MESH).start()

    held = (plane < planes // 2 - 1) | (plane > planes // 2)
    outward = jnp.where(plane < planes // 2, plane - 1, plane + 1)

    def own(q, t):
        return x_ref.at[:, :, q * tiles + t]

    def send_traces(q, t):
        pltpu.make_async_remote_copy(own(q, t), land.at[t, plane], column_out.at[t], column_in.at[t, plane],
                                     device_id={"shot": in_column(q)}, device_id_type=MESH).start()

    def send_all_traces(t):
        for q in range(planes):
            pl.when(q != plane)(lambda q=q: send_traces(q, t))

    for q in range(planes):
        pl.when(q < plane)(lambda q=q: send_traces(q, 0))
    above = jnp.minimum(plane + 1, planes - 1)
    ready = pltpu.make_async_copy(own(above, 0), first, first_in)
    ready.start()
    ready.wait()
    for q in range(planes):
        @pl.when(q > plane)
        def _(q=q):
            pl.semaphore_wait(near_column.at[q], 1)
            @pl.when(q == plane + 1)
            def _():
                pltpu.make_async_remote_copy(first, land.at[0, plane], column_out.at[0], column_in.at[0, plane],
                                             device_id={"shot": in_column(q)}, device_id_type=MESH).start()
            pl.when(q != plane + 1)(lambda: send_traces(q, 0))

    @pl.when(jnp.logical_not(held))
    def _():
        for t in range(1, tiles):
            send_all_traces(t)

    for t in range(tiles):
        pltpu.make_async_copy(own(plane, t), land.at[t, plane], own_in.at[t]).start()
    small = [pltpu.make_async_copy(row_hbm, row_ref, small_in.at[0]), pltpu.make_async_copy(wave_hbm, wave_ref, small_in.at[1])]
    for copy in small:
        copy.start()

    def share(t, q):
        for c in range(2):
            flat = land[t, q, :, c].astype(jnp.float32).reshape(shots * ROWS, points)
            for k in range(points // LANES):
                stage[c, k] = flat[:, k * LANES : (k + 1) * LANES]
        mine = rows_of(in_column(q))
        for c in range(2):
            for f in range(ROWS):
                for k in range(points // LANES):
                    traces[t, f, c, mine, pl.ds(k * LANES, LANES)] = (
                        stage[c, k, pl.ds(f, shots, stride=ROWS), :].astype(jnp.bfloat16))
        piece = traces.at[t, :, :, mine]
        for k in range(chips):
            pl.when(k != chip)(lambda k=k: send(piece, piece, chip_in.at[t, q, chip], in_plane(k)))
        send(piece, piece, core_in.at[t], sibling)

    pl.when(core == 0)(lambda: pl.semaphore_wait(near_core, 1))
    for k in range(chips):
        pl.when(k > chip)(lambda k=k: pl.semaphore_wait(near_chip.at[k], 1))

    @pl.loop(0, tiles)
    def _(t):
        pltpu.make_async_copy(land.at[t, plane], land.at[t, plane], own_in.at[t]).wait()
        share(t, plane)

    for copy in small:
        copy.wait()
    shot = lax.broadcasted_iota(jnp.int32, (points, points), 0)
    point = lax.broadcasted_iota(jnp.int32, (points, points), 1)
    eye[...] = jnp.where(shot == point, 1.0, 0.0).astype(jnp.bfloat16)
    mirrored = jnp.where(jnp.abs(shot - point) < row_ref[...], 1.0, 0.0).astype(jnp.bfloat16)
    keep[...] = turn(eye[...], mirrored)
    swap[...] = keep[...] * (1.0 - mirrored)

    def nearest_first(work):
        @pl.loop(1, planes)
        def _(d):
            pl.when(plane - d >= 0)(lambda: work(plane - d))
            pl.when(plane + d < planes)(lambda: work(plane + d))

    def from_columns(t):
        def one(q):
            pltpu.make_async_copy(land.at[t, q], land.at[t, q], column_in.at[t, q]).wait()
            share(t, q)

        nearest_first(one)

    def from_chips(t):
        def one(q):
            for k in range(chips):
                @pl.when(k != chip)
                def _(k=k):
                    piece = traces.at[t, :, :, rows_of(q * group + 2 * k + core)]
                    pltpu.make_async_copy(piece, piece, chip_in.at[t, q, k]).wait()
                    send(piece, piece, core_in.at[t], sibling)

        one(plane)
        nearest_first(one)
        half = traces.at[t, :, :, pl.ds(0, n // 2 * shots)]
        pltpu.make_async_copy(half, half, core_in.at[t]).wait()

    def fill(t):
        @pl.loop(0, ROWS)
        def _(f):
            for c in range(2):
                block = traces[t, f, c]
                filled[f, c] = block * keep[...] + turn(eye[...], block * swap[...])

    def multiply(t):
        height = planes * shots

        @pl.loop(0, ROWS)
        def _(f):
            left = jnp.concatenate(
                [filled[f, c, pl.ds(pl.multiple_of(in_column(q) * shots, shots), shots), :]
                 for c in range(2) for q in range(planes)], axis=0)
            dot = functools.partial(jnp.dot, preferred_element_type=jnp.float32)
            by_real, by_imag = dot(left, filled[f, 0]), dot(left, filled[f, 1])
            prod_real = by_real[:height] - by_imag[height:]
            prod_imag = by_imag[:height] + by_real[height:]
            which = (plane * tiles + t) * ROWS + f
            wave_real, wave_imag = wave_ref[0, which], wave_ref[1, which]
            out_real = -(wave_real * prod_real - wave_imag * prod_imag)
            out_imag = -(wave_real * prod_imag + wave_imag * prod_real)
            for q in range(points // LANES):
                lanes = slice(q * LANES, (q + 1) * LANES)
                ostage[0, q, pl.ds(f, height, stride=ROWS), :] = out_real[:, lanes]
                ostage[1, q, pl.ds(f, height, stride=ROWS), :] = out_imag[:, lanes]

        @pl.loop(0, planes)
        def _(z):
            rows = pl.ds(pl.multiple_of(z * shots * ROWS, shots * ROWS), shots * ROWS)
            for c in range(2):
                for q in range(points // LANES):
                    block = ostage[c, q, rows, :].reshape(shots, ROWS, LANES)
                    out[t, z, :, c, :, pl.ds(q * LANES, LANES)] = block.astype(jnp.bfloat16)

    def send_results(t):
        theirs = o_ref.at[:, :, plane * tiles + t]
        for q in range(planes):
            @pl.when(q != plane)
            def _(q=q):
                pltpu.make_async_remote_copy(out.at[t, q], theirs, out_send, out_recv,
                                             device_id={"shot": in_column(q)}, device_id_type=MESH).start()
        pltpu.make_async_copy(out.at[t, plane], theirs, own_out.at[t]).start()

    @pl.loop(0, tiles)
    def _(t):
        from_columns(t)
        sent = land.at[t, pl.ds(0, planes - 1)]
        pltpu.make_async_copy(sent, sent, column_out.at[t]).wait()
        pl.when((plane > 0) & (plane < planes - 1))(lambda: signal(go.at[t], in_column(outward)))

        @pl.when(held)
        def _():
            pl.semaphore_wait(go.at[t], 1)
            pl.when(t > 0)(lambda: send_results(t - 1))
            pl.when(t < tiles - 1)(lambda: send_all_traces(t + 1))

        from_chips(t)
        fill(t)
        multiply(t)
        pl.when((t == tiles - 1) | jnp.logical_not(held))(lambda: send_results(t))

    for t in range(tiles):
        pltpu.make_async_copy(out.at[t, 0], o_ref.at[:, :, t], own_out.at[t]).wait()
    shared = traces.at[:, :, :, pl.ds(0, (n - planes) * shots)]
    pltpu.make_async_copy(shared, shared, in_send).wait()
    others = o_ref.at[:, :, pl.ds(0, (planes - 1) * tiles)]
    pltpu.make_async_copy(others, others, out_send).wait()
    pltpu.make_async_copy(others, others, out_recv).wait()


def shards(n, spectra, fold_counts, inverse_wavelet):
    shots, _, bins, points = spectra.shape
    bf16, f32 = jnp.bfloat16, jnp.float32
    tiles = 2
    planes = bins // (tiles * ROWS)
    tiled = (shots, 2, bins // ROWS, ROWS, points)
    height = planes * shots
    landed = pl.pallas_call(
        functools.partial(kernel, planes, n),
        out_shape=pltpu.VMEM(tiled, bf16),
        in_specs=[pl.BlockSpec(memory_space=pl.ANY)] * 3,
        out_specs=pl.BlockSpec(memory_space=pltpu.VMEM),
        scratch_shapes=[
            pltpu.VMEM((tiles, planes, shots, 2, ROWS, points), bf16),
            pltpu.VMEM((2, points // LANES, shots * ROWS, LANES), f32),
            pltpu.VMEM((tiles, ROWS, 2, points, points), bf16),
            pltpu.VMEM((ROWS, 2, points, points), bf16),
            pltpu.VMEM((2, points // LANES, height * ROWS, LANES), f32),
            pltpu.VMEM((tiles, planes, shots, 2, ROWS, points), bf16),
            pltpu.VMEM((points, points), bf16),
            pltpu.VMEM((points, points), bf16),
            pltpu.VMEM((points, points), bf16),
            pltpu.VMEM((1, points), jnp.int32),
            pltpu.SMEM((2, bins), f32),
            pltpu.SemaphoreType.REGULAR((planes,)),
            pltpu.SemaphoreType.REGULAR,
            pltpu.SemaphoreType.REGULAR((n // planes // 2,)),
            pltpu.SemaphoreType.REGULAR((tiles,)),
            pltpu.VMEM((shots, 2, ROWS, points), bf16),
            pltpu.SemaphoreType.DMA,
            pltpu.SemaphoreType.DMA((2,)),
            pltpu.SemaphoreType.DMA((tiles,)),
            pltpu.SemaphoreType.DMA,
            pltpu.SemaphoreType.DMA((tiles,)),
            pltpu.SemaphoreType.DMA((tiles, planes)),
            pltpu.SemaphoreType.DMA((tiles, planes, n // planes // 2)),
            pltpu.SemaphoreType.DMA((tiles,)),
            pltpu.SemaphoreType.DMA((tiles,)),
            pltpu.SemaphoreType.DMA,
            pltpu.SemaphoreType.DMA,
        ],
        compiler_params=pltpu.CompilerParams(
            collective_id=0, has_side_effects=True, vmem_limit_bytes=VMEM_BYTES),
    )(spectra.reshape(tiled), fold_counts[None, :], inverse_wavelet)
    return landed.reshape(spectra.shape)


def solution(mesh):
    spec = P(("groups", "shot"), None, None, None)
    return jax.shard_map(functools.partial(shards, mesh.shape["shot"]), mesh=mesh,
                         in_specs=(spec, P("groups"), P()), out_specs=spec, check_vma=False)
```

```python
import functools

import jax
import jax.numpy as jnp
from jax import lax
from jax.experimental import pallas as pl
from jax.experimental.pallas import tpu as pltpu
from jax.sharding import PartitionSpec as P

MESH = pl.DeviceIdType.MESH
VMEM_BYTES = 50 * 1024 * 1024
ROWS = 8
LANES = 128


def turn(eye, block):
    return lax.dot_general(eye, block, (((1,), (1,)), ((), ())),
                           preferred_element_type=jnp.float32).astype(jnp.bfloat16)


def kernel(planes, n, x_ref, row_hbm, wave_hbm, o_ref,
           land, stage, traces, filled, ostage, out, keep, swap, eye, row_ref, wave_ref,
           near_column, near_core, near_chip, go,
           first, first_in, small_in, own_in, in_send, column_out, column_in, chip_in, core_in, own_out, out_send, out_recv):
    shots, _, _, _, points = x_ref.shape
    tiles = land.shape[0]
    group = n // planes
    chips = group // 2
    me = lax.axis_index("shot")
    plane, place = me // group, lax.rem(me, group)
    chip, core = place // 2, lax.rem(place, 2)
    sibling = me + 1 - 2 * core

    def in_column(q):
        return q * group + place

    def in_plane(k):
        return plane * group + 2 * k + core

    def signal(sem, to):
        pl.semaphore_signal(sem, inc=1, device_id={"shot": to}, device_id_type=MESH)

    barrier = pltpu.get_barrier_semaphore()
    for q in range(planes):
        pl.when(q > plane)(lambda q=q: signal(barrier, in_column(q)))
    pl.when(core == 1)(lambda: signal(barrier, sibling))
    for k in range(chips):
        pl.when(k > chip)(lambda k=k: signal(barrier, in_plane(k)))
    lower = plane + 1 - core + chip
    pl.when(lower > 0)(lambda: pl.semaphore_wait(barrier, lower))
    for q in range(planes):
        pl.when(q < plane)(lambda q=q: signal(near_column.at[plane], in_column(q)))
    pl.when(core == 0)(lambda: signal(near_core, sibling))
    for k in range(chips):
        pl.when(k < chip)(lambda k=k: signal(near_chip.at[chip], in_plane(k)))

    def rows_of(source):
        return pl.ds(pl.multiple_of(source * shots, shots), shots)

    def send(src, dst, sem, to):
        pltpu.make_async_remote_copy(src, dst, in_send, sem, device_id={"shot": to}, device_id_type=MESH).start()

    held = (plane < planes // 2 - 1) | (plane > planes // 2)
    outward = jnp.where(plane < planes // 2, plane - 1, plane + 1)

    def own(q, t):
        return x_ref.at[:, :, q * tiles + t]

    def send_traces(q, t):
        pltpu.make_async_remote_copy(own(q, t), land.at[t, plane], column_out.at[t], column_in.at[t, plane],
                                     device_id={"shot": in_column(q)}, device_id_type=MESH).start()

    def send_all_traces(t):
        for q in range(planes):
            pl.when(q != plane)(lambda q=q: send_traces(q, t))

    for q in range(planes):
        pl.when(q < plane)(lambda q=q: send_traces(q, 0))
    above = jnp.minimum(plane + 1, planes - 1)
    ready = pltpu.make_async_copy(own(above, 0), first, first_in)
    ready.start()
    ready.wait()
    for q in range(planes):
        @pl.when(q > plane)
        def _(q=q):
            pl.semaphore_wait(near_column.at[q], 1)
            @pl.when(q == plane + 1)
            def _():
                pltpu.make_async_remote_copy(first, land.at[0, plane], column_out.at[0], column_in.at[0, plane],
                                             device_id={"shot": in_column(q)}, device_id_type=MESH).start()
            pl.when(q != plane + 1)(lambda: send_traces(q, 0))

    @pl.when(jnp.logical_not(held))
    def _():
        for t in range(1, tiles):
            send_all_traces(t)

    for t in range(tiles):
        pltpu.make_async_copy(own(plane, t), land.at[t, plane], own_in.at[t]).start()
    small = [pltpu.make_async_copy(row_hbm, row_ref, small_in.at[0]), pltpu.make_async_copy(wave_hbm, wave_ref, small_in.at[1])]
    for copy in small:
        copy.start()

    def share(t, q):
        for c in range(2):
            flat = land[t, q, :, c].astype(jnp.float32).reshape(shots * ROWS, points)
            for k in range(points // LANES):
                stage[c, k] = flat[:, k * LANES : (k + 1) * LANES]
        mine = rows_of(in_column(q))
        for c in range(2):
            for f in range(ROWS):
                for k in range(points // LANES):
                    traces[t, f, c, mine, pl.ds(k * LANES, LANES)] = (
                        stage[c, k, pl.ds(f, shots, stride=ROWS), :].astype(jnp.bfloat16))
        piece = traces.at[t, :, :, mine]
        for k in range(chips):
            pl.when(k != chip)(lambda k=k: send(piece, piece, chip_in.at[t, q, chip], in_plane(k)))
        send(piece, piece, core_in.at[t], sibling)

    pl.when(core == 1)(lambda: pl.semaphore_wait(near_core, 1))
    for k in range(chips):
        pl.when(k > chip)(lambda k=k: pl.semaphore_wait(near_chip.at[k], 1))

    @pl.loop(0, tiles)
    def _(t):
        pltpu.make_async_copy(land.at[t, plane], land.at[t, plane], own_in.at[t]).wait()
        share(t, plane)

    for copy in small:
        copy.wait()
    shot = lax.broadcasted_iota(jnp.int32, (points, points), 0)
    point = lax.broadcasted_iota(jnp.int32, (points, points), 1)
    eye[...] = jnp.where(shot == point, 1.0, 0.0).astype(jnp.bfloat16)
    mirrored = jnp.where(jnp.abs(shot - point) < row_ref[...], 1.0, 0.0).astype(jnp.bfloat16)
    keep[...] = turn(eye[...], mirrored)
    swap[...] = keep[...] * (1.0 - mirrored)

    def nearest_first(work):
        @pl.loop(1, planes)
        def _(d):
            pl.when(plane - d >= 0)(lambda: work(plane - d))
            pl.when(plane + d < planes)(lambda: work(plane + d))

    def from_columns(t):
        def one(q):
            pltpu.make_async_copy(land.at[t, q], land.at[t, q], column_in.at[t, q]).wait()
            share(t, q)

        nearest_first(one)

    def from_chips(t):
        def one(q):
            for k in range(chips):
                @pl.when(k != chip)
                def _(k=k):
                    piece = traces.at[t, :, :, rows_of(q * group + 2 * k + core)]
                    pltpu.make_async_copy(piece, piece, chip_in.at[t, q, k]).wait()
                    send(piece, piece, core_in.at[t], sibling)

        one(plane)
        nearest_first(one)
        half = traces.at[t, :, :, pl.ds(0, n // 2 * shots)]
        pltpu.make_async_copy(half, half, core_in.at[t]).wait()

    def fill(t):
        @pl.loop(0, ROWS)
        def _(f):
            for c in range(2):
                block = traces[t, f, c]
                filled[f, c] = block * keep[...] + turn(eye[...], block * swap[...])

    def multiply(t):
        height = planes * shots

        @pl.loop(0, ROWS)
        def _(f):
            left = jnp.concatenate(
                [filled[f, c, pl.ds(pl.multiple_of(in_column(q) * shots, shots), shots), :]
                 for c in range(2) for q in range(planes)], axis=0)
            dot = functools.partial(jnp.dot, preferred_element_type=jnp.float32)
            by_real, by_imag = dot(left, filled[f, 0]), dot(left, filled[f, 1])
            prod_real = by_real[:height] - by_imag[height:]
            prod_imag = by_imag[:height] + by_real[height:]
            which = (plane * tiles + t) * ROWS + f
            wave_real, wave_imag = wave_ref[0, which], wave_ref[1, which]
            out_real = -(wave_real * prod_real - wave_imag * prod_imag)
            out_imag = -(wave_real * prod_imag + wave_imag * prod_real)
            for q in range(points // LANES):
                lanes = slice(q * LANES, (q + 1) * LANES)
                ostage[0, q, pl.ds(f, height, stride=ROWS), :] = out_real[:, lanes]
                ostage[1, q, pl.ds(f, height, stride=ROWS), :] = out_imag[:, lanes]

        @pl.loop(0, planes)
        def _(z):
            rows = pl.ds(pl.multiple_of(z * shots * ROWS, shots * ROWS), shots * ROWS)
            for c in range(2):
                for q in range(points // LANES):
                    block = ostage[c, q, rows, :].reshape(shots, ROWS, LANES)
                    out[t, z, :, c, :, pl.ds(q * LANES, LANES)] = block.astype(jnp.bfloat16)

    def send_results(t):
        theirs = o_ref.at[:, :, plane * tiles + t]
        for q in range(planes):
            @pl.when(q != plane)
            def _(q=q):
                pltpu.make_async_remote_copy(out.at[t, q], theirs, out_send, out_recv,
                                             device_id={"shot": in_column(q)}, device_id_type=MESH).start()
        pltpu.make_async_copy(out.at[t, plane], theirs, own_out.at[t]).start()

    @pl.loop(0, tiles)
    def _(t):
        from_columns(t)
        sent = land.at[t, pl.ds(0, planes - 1)]
        pltpu.make_async_copy(sent, sent, column_out.at[t]).wait()
        pl.when((plane > 0) & (plane < planes - 1))(lambda: signal(go.at[t], in_column(outward)))

        @pl.when(held)
        def _():
            pl.semaphore_wait(go.at[t], 1)
            pl.when(t > 0)(lambda: send_results(t - 1))
            pl.when(t < tiles - 1)(lambda: send_all_traces(t + 1))

        from_chips(t)
        fill(t)
        multiply(t)
        pl.when((t == tiles - 1) | jnp.logical_not(held))(lambda: send_results(t))

    for t in range(tiles):
        pltpu.make_async_copy(out.at[t, 0], o_ref.at[:, :, t], own_out.at[t]).wait()
    shared = traces.at[:, :, :, pl.ds(0, (n - planes) * shots)]
    pltpu.make_async_copy(shared, shared, in_send).wait()
    others = o_ref.at[:, :, pl.ds(0, (planes - 1) * tiles)]
    pltpu.make_async_copy(others, others, out_send).wait()
    pltpu.make_async_copy(others, others, out_recv).wait()


def shards(n, spectra, fold_counts, inverse_wavelet):
    shots, _, bins, points = spectra.shape
    bf16, f32 = jnp.bfloat16, jnp.float32
    tiles = 2
    planes = bins // (tiles * ROWS)
    tiled = (shots, 2, bins // ROWS, ROWS, points)
    height = planes * shots
    landed = pl.pallas_call(
        functools.partial(kernel, planes, n),
        out_shape=pltpu.VMEM(tiled, bf16),
        in_specs=[pl.BlockSpec(memory_space=pl.ANY)] * 3,
        out_specs=pl.BlockSpec(memory_space=pltpu.VMEM),
        scratch_shapes=[
            pltpu.VMEM((tiles, planes, shots, 2, ROWS, points), bf16),
            pltpu.VMEM((2, points // LANES, shots * ROWS, LANES), f32),
            pltpu.VMEM((tiles, ROWS, 2, points, points), bf16),
            pltpu.VMEM((ROWS, 2, points, points), bf16),
            pltpu.VMEM((2, points // LANES, height * ROWS, LANES), f32),
            pltpu.VMEM((tiles, planes, shots, 2, ROWS, points), bf16),
            pltpu.VMEM((points, points), bf16),
            pltpu.VMEM((points, points), bf16),
            pltpu.VMEM((points, points), bf16),
            pltpu.VMEM((1, points), jnp.int32),
            pltpu.SMEM((2, bins), f32),
            pltpu.SemaphoreType.REGULAR((planes,)),
            pltpu.SemaphoreType.REGULAR,
            pltpu.SemaphoreType.REGULAR((n // planes // 2,)),
            pltpu.SemaphoreType.REGULAR((tiles,)),
            pltpu.VMEM((shots, 2, ROWS, points), bf16),
            pltpu.SemaphoreType.DMA,
            pltpu.SemaphoreType.DMA((2,)),
            pltpu.SemaphoreType.DMA((tiles,)),
            pltpu.SemaphoreType.DMA,
            pltpu.SemaphoreType.DMA((tiles,)),
            pltpu.SemaphoreType.DMA((tiles, planes)),
            pltpu.SemaphoreType.DMA((tiles, planes, n // planes // 2)),
            pltpu.SemaphoreType.DMA((tiles,)),
            pltpu.SemaphoreType.DMA((tiles,)),
            pltpu.SemaphoreType.DMA,
            pltpu.SemaphoreType.DMA,
        ],
        compiler_params=pltpu.CompilerParams(
            collective_id=0, has_side_effects=True, vmem_limit_bytes=VMEM_BYTES),
    )(spectra.reshape(tiled), fold_counts[None, :], inverse_wavelet)
    return landed.reshape(spectra.shape)


def solution(mesh):
    spec = P(("groups", "shot"), None, None, None)
    return jax.shard_map(functools.partial(shards, mesh.shape["shot"]), mesh=mesh,
                         in_specs=(spec, P("groups"), P()), out_specs=spec, check_vma=False)
```

```python
import functools

import jax
import jax.numpy as jnp
from jax import lax
from jax.experimental import pallas as pl
from jax.experimental.pallas import tpu as pltpu
from jax.sharding import PartitionSpec as P

MESH = pl.DeviceIdType.MESH
VMEM_BYTES = 50 * 1024 * 1024
ROWS = 8
LANES = 128


def turn(eye, block):
    return lax.dot_general(eye, block, (((1,), (1,)), ((), ())),
                           preferred_element_type=jnp.float32).astype(jnp.bfloat16)


def kernel(planes, n, x_ref, row_hbm, wave_hbm, o_ref,
           land, stage, traces, filled, ostage, out, keep, swap, eye, row_ref, wave_ref,
           near_column, near_core, near_chip, go,
           first, first_in, small_in, own_in, in_send, column_out, column_in, chip_in, core_in, out_send, out_recv):
    shots, _, _, _, points = x_ref.shape
    tiles = land.shape[0]
    group = n // planes
    chips = group // 2
    me = lax.axis_index("shot")
    plane, place = me // group, lax.rem(me, group)
    chip, core = place // 2, lax.rem(place, 2)
    sibling = me + 1 - 2 * core

    def in_column(q):
        return q * group + place

    def in_plane(k):
        return plane * group + 2 * k + core

    def signal(sem, to):
        pl.semaphore_signal(sem, inc=1, device_id={"shot": to}, device_id_type=MESH)

    above = jnp.minimum(plane + 1, planes - 1)
    ready = pltpu.make_async_copy(x_ref.at[:, :, above * tiles], first, first_in)
    ready.start()

    barrier = pltpu.get_barrier_semaphore()
    for q in range(planes):
        pl.when(q > plane)(lambda q=q: signal(barrier, in_column(q)))
    pl.when(core == 1)(lambda: signal(barrier, sibling))
    for k in range(chips):
        pl.when(k > chip)(lambda k=k: signal(barrier, in_plane(k)))
    lower = plane + 1 - core + chip
    pl.when(lower > 0)(lambda: pl.semaphore_wait(barrier, lower))
    for q in range(planes):
        pl.when(q < plane)(lambda q=q: signal(near_column.at[plane], in_column(q)))
    pl.when(core == 0)(lambda: signal(near_core, sibling))
    for k in range(chips):
        pl.when(k < chip)(lambda k=k: signal(near_chip.at[chip], in_plane(k)))

    def rows_of(source):
        return pl.ds(pl.multiple_of(source * shots, shots), shots)

    def send(src, dst, sem, to):
        pltpu.make_async_remote_copy(src, dst, in_send, sem, device_id={"shot": to}, device_id_type=MESH).start()

    held = (plane < planes // 2 - 1) | (plane > planes // 2)
    outward = jnp.where(plane < planes // 2, plane - 1, plane + 1)

    def own(q, t):
        return x_ref.at[:, :, q * tiles + t]

    def send_traces(q, t):
        pltpu.make_async_remote_copy(own(q, t), land.at[t, plane], column_out.at[t], column_in.at[t, plane],
                                     device_id={"shot": in_column(q)}, device_id_type=MESH).start()

    def send_all_traces(t):
        for q in range(planes):
            pl.when(q != plane)(lambda q=q: send_traces(q, t))

    for q in range(planes):
        pl.when(q < plane)(lambda q=q: send_traces(q, 0))
    ready.wait()
    for q in range(planes):
        @pl.when(q > plane)
        def _(q=q):
            pl.semaphore_wait(near_column.at[q], 1)
            @pl.when(q == plane + 1)
            def _():
                pltpu.make_async_remote_copy(first, land.at[0, plane], column_out.at[0], column_in.at[0, plane],
                                             device_id={"shot": in_column(q)}, device_id_type=MESH).start()
            pl.when(q != plane + 1)(lambda: send_traces(q, 0))

    @pl.when(jnp.logical_not(held))
    def _():
        for t in range(1, tiles):
            send_all_traces(t)

    for t in range(tiles):
        pltpu.make_async_copy(own(plane, t), land.at[t, plane], own_in.at[t]).start()
    small = [pltpu.make_async_copy(row_hbm, row_ref, first_in), pltpu.make_async_copy(wave_hbm, wave_ref, small_in)]
    for copy in small:
        copy.start()

    def share(t, q):
        for c in range(2):
            flat = land[t, q, :, c].astype(jnp.float32).reshape(shots * ROWS, points)
            for k in range(points // LANES):
                stage[c, k] = flat[:, k * LANES : (k + 1) * LANES]
        mine = rows_of(in_column(q))
        for c in range(2):
            for f in range(ROWS):
                for k in range(points // LANES):
                    traces[t, f, c, mine, pl.ds(k * LANES, LANES)] = (
                        stage[c, k, pl.ds(f, shots, stride=ROWS), :].astype(jnp.bfloat16))
        piece = traces.at[t, :, :, mine]
        for k in range(chips):
            pl.when(k != chip)(lambda k=k: send(piece, piece, chip_in.at[t], in_plane(k)))
        send(piece, piece, core_in.at[t], sibling)

    pl.when(core == 1)(lambda: pl.semaphore_wait(near_core, 1))
    for k in range(chips):
        pl.when(k > chip)(lambda k=k: pl.semaphore_wait(near_chip.at[k], 1))

    @pl.loop(0, tiles)
    def _(t):
        pltpu.make_async_copy(land.at[t, plane], land.at[t, plane], own_in.at[t]).wait()
        share(t, plane)

    for copy in small:
        copy.wait()
    shot = lax.broadcasted_iota(jnp.int32, (points, points), 0)
    point = lax.broadcasted_iota(jnp.int32, (points, points), 1)
    eye[...] = jnp.where(shot == point, 1.0, 0.0).astype(jnp.bfloat16)
    mirrored = jnp.where(jnp.abs(shot - point) < row_ref[...], 1.0, 0.0).astype(jnp.bfloat16)
    keep[...] = turn(eye[...], mirrored)
    swap[...] = keep[...] * (1.0 - mirrored)

    def nearest_first(work):
        @pl.loop(1, planes)
        def _(d):
            pl.when(plane - d >= 0)(lambda: work(plane - d))
            pl.when(plane + d < planes)(lambda: work(plane + d))

    def from_columns(t):
        def one(q):
            pltpu.make_async_copy(land.at[t, q], land.at[t, q], column_in.at[t, q]).wait()
            share(t, q)

        nearest_first(one)

    def from_chips(t):
        if chips > 1:
            came = traces.at[t, :, :, pl.ds(0, planes * (chips - 1) * shots)]
            pltpu.make_async_copy(came, came, chip_in.at[t]).wait()

            @pl.loop(0, planes)
            def _(q):
                for k in range(chips):
                    @pl.when(k != chip)
                    def _(k=k):
                        piece = traces.at[t, :, :, rows_of(q * group + 2 * k + core)]
                        send(piece, piece, core_in.at[t], sibling)

        half = traces.at[t, :, :, pl.ds(0, n // 2 * shots)]
        pltpu.make_async_copy(half, half, core_in.at[t]).wait()

    def fill(t):
        @pl.loop(0, ROWS)
        def _(f):
            for c in range(2):
                block = traces[t, f, c]
                filled[f, c] = block * keep[...] + turn(eye[...], block * swap[...])

    def multiply(t):
        height = planes * shots

        @pl.loop(0, ROWS)
        def _(f):
            left = jnp.concatenate(
                [filled[f, c, pl.ds(pl.multiple_of(in_column(q) * shots, shots), shots), :]
                 for c in range(2) for q in range(planes)], axis=0)
            dot = functools.partial(jnp.dot, preferred_element_type=jnp.float32)
            by_real, by_imag = dot(left, filled[f, 0]), dot(left, filled[f, 1])
            prod_real = by_real[:height] - by_imag[height:]
            prod_imag = by_imag[:height] + by_real[height:]
            which = (plane * tiles + t) * ROWS + f
            wave_real, wave_imag = wave_ref[0, which], wave_ref[1, which]
            out_real = -(wave_real * prod_real - wave_imag * prod_imag)
            out_imag = -(wave_real * prod_imag + wave_imag * prod_real)
            for q in range(points // LANES):
                lanes = slice(q * LANES, (q + 1) * LANES)
                ostage[0, q, pl.ds(f, height, stride=ROWS), :] = out_real[:, lanes]
                ostage[1, q, pl.ds(f, height, stride=ROWS), :] = out_imag[:, lanes]

        @pl.loop(0, planes)
        def _(z):
            rows = pl.ds(pl.multiple_of(z * shots * ROWS, shots * ROWS), shots * ROWS)
            for c in range(2):
                for q in range(points // LANES):
                    block = ostage[c, q, rows, :].reshape(shots, ROWS, LANES)
                    out[t, z, :, c, :, pl.ds(q * LANES, LANES)] = block.astype(jnp.bfloat16)

    def send_results(t):
        theirs = o_ref.at[:, :, plane * tiles + t]
        for q in range(planes):
            @pl.when(q != plane)
            def _(q=q):
                pltpu.make_async_remote_copy(out.at[t, q], theirs, out_send, out_recv,
                                             device_id={"shot": in_column(q)}, device_id_type=MESH).start()
        pltpu.make_async_copy(out.at[t, plane], theirs, own_in.at[t]).start()

    @pl.loop(0, tiles)
    def _(t):
        from_columns(t)
        sent = land.at[t, pl.ds(0, planes - 1)]
        pltpu.make_async_copy(sent, sent, column_out.at[t]).wait()
        pl.when((plane > 0) & (plane < planes - 1))(lambda: signal(go, in_column(outward)))

        @pl.when(held)
        def _():
            pl.semaphore_wait(go, 1)
            pl.when(t > 0)(lambda: send_results(t - 1))
            pl.when(t < tiles - 1)(lambda: send_all_traces(t + 1))

        from_chips(t)
        fill(t)
        multiply(t)
        pl.when((t == tiles - 1) | jnp.logical_not(held))(lambda: send_results(t))

    for t in range(tiles):
        pltpu.make_async_copy(out.at[t, 0], o_ref.at[:, :, t], own_in.at[t]).wait()
    shared = traces.at[:, :, :, pl.ds(0, (n - planes) * shots)]
    pltpu.make_async_copy(shared, shared, in_send).wait()
    others = o_ref.at[:, :, pl.ds(0, (planes - 1) * tiles)]
    pltpu.make_async_copy(others, others, out_send).wait()
    pltpu.make_async_copy(others, others, out_recv).wait()


def shards(n, spectra, fold_counts, inverse_wavelet):
    shots, _, bins, points = spectra.shape
    bf16, f32 = jnp.bfloat16, jnp.float32
    tiles = 2
    planes = bins // (tiles * ROWS)
    tiled = (shots, 2, bins // ROWS, ROWS, points)
    height = planes * shots
    landed = pl.pallas_call(
        functools.partial(kernel, planes, n),
        out_shape=pltpu.VMEM(tiled, bf16),
        in_specs=[pl.BlockSpec(memory_space=pl.ANY)] * 3,
        out_specs=pl.BlockSpec(memory_space=pltpu.VMEM),
        scratch_shapes=[
            pltpu.VMEM((tiles, planes, shots, 2, ROWS, points), bf16),
            pltpu.VMEM((2, points // LANES, shots * ROWS, LANES), f32),
            pltpu.VMEM((tiles, ROWS, 2, points, points), bf16),
            pltpu.VMEM((ROWS, 2, points, points), bf16),
            pltpu.VMEM((2, points // LANES, height * ROWS, LANES), f32),
            pltpu.VMEM((tiles, planes, shots, 2, ROWS, points), bf16),
            pltpu.VMEM((points, points), bf16),
            pltpu.VMEM((points, points), bf16),
            pltpu.VMEM((points, points), bf16),
            pltpu.VMEM((1, points), jnp.int32),
            pltpu.SMEM((2, bins), f32),
            pltpu.SemaphoreType.REGULAR((planes,)),
            pltpu.SemaphoreType.REGULAR,
            pltpu.SemaphoreType.REGULAR((n // planes // 2,)),
            pltpu.SemaphoreType.REGULAR,
            pltpu.VMEM((shots, 2, ROWS, points), bf16),
            pltpu.SemaphoreType.DMA,
            pltpu.SemaphoreType.DMA,
            pltpu.SemaphoreType.DMA((tiles,)),
            pltpu.SemaphoreType.DMA,
            pltpu.SemaphoreType.DMA((tiles,)),
            pltpu.SemaphoreType.DMA((tiles, planes)),
            pltpu.SemaphoreType.DMA((tiles,)),
            pltpu.SemaphoreType.DMA((tiles,)),
            pltpu.SemaphoreType.DMA,
            pltpu.SemaphoreType.DMA,
        ],
        compiler_params=pltpu.CompilerParams(
            collective_id=0, has_side_effects=True, vmem_limit_bytes=VMEM_BYTES),
    )(spectra.reshape(tiled), fold_counts[None, :], inverse_wavelet)
    return landed.reshape(spectra.shape)


def solution(mesh):
    spec = P(("groups", "shot"), None, None, None)
    return jax.shard_map(functools.partial(shards, mesh.shape["shot"]), mesh=mesh,
                         in_specs=(spec, P("groups"), P()), out_specs=spec, check_vma=False)
```

```python
import functools

import jax
import jax.numpy as jnp
from jax import lax
from jax.experimental import pallas as pl
from jax.experimental.pallas import tpu as pltpu
from jax.sharding import PartitionSpec as P

MESH = pl.DeviceIdType.MESH
VMEM_BYTES = 50 * 1024 * 1024
ROWS = 8
LANES = 128


def turn(eye, block):
    return lax.dot_general(eye, block, (((1,), (1,)), ((), ())),
                           preferred_element_type=jnp.float32).astype(jnp.bfloat16)


def kernel(planes, n, x_ref, row_hbm, wave_hbm, o_ref,
           land, stage, traces, filled, ostage, out, keep, swap, eye, row_ref, wave_ref,
           near_column, near_core, near_chip, go,
           first, first_in, small_in, own_in, in_send, column_out, column_in, chip_in, core_in, out_send, out_recv):
    shots, _, _, _, points = x_ref.shape
    tiles = land.shape[0]
    group = n // planes
    chips = group // 2
    me = lax.axis_index("shot")
    plane, place = me // group, lax.rem(me, group)
    chip, core = place // 2, lax.rem(place, 2)
    sibling = me + 1 - 2 * core

    def in_column(q):
        return q * group + place

    def in_plane(k):
        return plane * group + 2 * k + core

    def signal(sem, to):
        pl.semaphore_signal(sem, inc=1, device_id={"shot": to}, device_id_type=MESH)

    above = jnp.minimum(plane + 1, planes - 1)
    ready = pltpu.make_async_copy(x_ref.at[:, :, above * tiles], first, first_in)
    ready.start()

    barrier = pltpu.get_barrier_semaphore()
    pl.loop(plane + 1, planes)(lambda q: signal(barrier, in_column(q)))
    pl.when(core == 1)(lambda: signal(barrier, sibling))
    pl.loop(chip + 1, chips)(lambda k: signal(barrier, in_plane(k)))
    lower = plane + 1 - core + chip
    pl.when(lower > 0)(lambda: pl.semaphore_wait(barrier, lower))
    pl.loop(0, plane)(lambda q: signal(near_column.at[plane], in_column(q)))
    pl.when(core == 0)(lambda: signal(near_core, sibling))
    pl.loop(0, chip)(lambda k: signal(near_chip.at[chip], in_plane(k)))

    def rows_of(source):
        return pl.ds(pl.multiple_of(source * shots, shots), shots)

    def send(src, dst, sem, to):
        pltpu.make_async_remote_copy(src, dst, in_send, sem, device_id={"shot": to}, device_id_type=MESH).start()

    held = (plane < planes // 2 - 1) | (plane > planes // 2)
    outward = jnp.where(plane < planes // 2, plane - 1, plane + 1)

    def own(q, t):
        return x_ref.at[:, :, q * tiles + t]

    def send_traces(q, t):
        pltpu.make_async_remote_copy(own(q, t), land.at[t, plane], column_out.at[t], column_in.at[t, plane],
                                     device_id={"shot": in_column(q)}, device_id_type=MESH).start()

    def send_all_traces(t):
        @pl.loop(0, planes)
        def _(q):
            pl.when(q != plane)(lambda: send_traces(q, t))

    pl.loop(0, plane)(lambda q: send_traces(q, 0))
    ready.wait()

    @pl.loop(plane + 1, planes)
    def _(q):
        pl.semaphore_wait(near_column.at[q], 1)

        @pl.when(q == plane + 1)
        def _():
            pltpu.make_async_remote_copy(first, land.at[0, plane], column_out.at[0], column_in.at[0, plane],
                                         device_id={"shot": in_column(q)}, device_id_type=MESH).start()

        pl.when(q > plane + 1)(lambda: send_traces(q, 0))

    @pl.when(jnp.logical_not(held))
    def _():
        for t in range(1, tiles):
            send_all_traces(t)

    for t in range(tiles):
        pltpu.make_async_copy(own(plane, t), land.at[t, plane], own_in.at[t]).start()
    small = [pltpu.make_async_copy(row_hbm, row_ref, first_in), pltpu.make_async_copy(wave_hbm, wave_ref, small_in)]
    for copy in small:
        copy.start()

    def share(t, q):
        for c in range(2):
            flat = land[t, q, :, c].astype(jnp.float32).reshape(shots * ROWS, points)
            for k in range(points // LANES):
                stage[c, k] = flat[:, k * LANES : (k + 1) * LANES]
        mine = rows_of(in_column(q))
        for c in range(2):
            for f in range(ROWS):
                for k in range(points // LANES):
                    traces[t, f, c, mine, pl.ds(k * LANES, LANES)] = (
                        stage[c, k, pl.ds(f, shots, stride=ROWS), :].astype(jnp.bfloat16))
        piece = traces.at[t, :, :, mine]
        for k in range(chips):
            pl.when(k != chip)(lambda k=k: send(piece, piece, chip_in.at[t], in_plane(k)))
        send(piece, piece, core_in.at[t], sibling)

    pl.when(core == 1)(lambda: pl.semaphore_wait(near_core, 1))
    for k in range(chips):
        pl.when(k > chip)(lambda k=k: pl.semaphore_wait(near_chip.at[k], 1))

    @pl.loop(0, tiles)
    def _(t):
        pltpu.make_async_copy(land.at[t, plane], land.at[t, plane], own_in.at[t]).wait()
        share(t, plane)

    for copy in small:
        copy.wait()
    shot = lax.broadcasted_iota(jnp.int32, (points, points), 0)
    point = lax.broadcasted_iota(jnp.int32, (points, points), 1)
    eye[...] = jnp.where(shot == point, 1.0, 0.0).astype(jnp.bfloat16)
    mirrored = jnp.where(jnp.abs(shot - point) < row_ref[...], 1.0, 0.0).astype(jnp.bfloat16)
    keep[...] = turn(eye[...], mirrored)
    swap[...] = keep[...] * (1.0 - mirrored)

    def nearest_first(work):
        @pl.loop(1, planes)
        def _(d):
            pl.when(plane - d >= 0)(lambda: work(plane - d))
            pl.when(plane + d < planes)(lambda: work(plane + d))

    def from_columns(t):
        def one(q):
            pltpu.make_async_copy(land.at[t, q], land.at[t, q], column_in.at[t, q]).wait()
            share(t, q)

        nearest_first(one)

    def from_chips(t):
        if chips > 1:
            came = traces.at[t, :, :, pl.ds(0, planes * (chips - 1) * shots)]
            pltpu.make_async_copy(came, came, chip_in.at[t]).wait()

            @pl.loop(0, planes)
            def _(q):
                for k in range(chips):
                    @pl.when(k != chip)
                    def _(k=k):
                        piece = traces.at[t, :, :, rows_of(q * group + 2 * k + core)]
                        send(piece, piece, core_in.at[t], sibling)

        half = traces.at[t, :, :, pl.ds(0, n // 2 * shots)]
        pltpu.make_async_copy(half, half, core_in.at[t]).wait()

    def fill(t):
        @pl.loop(0, ROWS)
        def _(f):
            for c in range(2):
                block = traces[t, f, c]
                filled[f, c] = block * keep[...] + turn(eye[...], block * swap[...])

    def multiply(t):
        height = planes * shots

        @pl.loop(0, ROWS)
        def _(f):
            left = jnp.concatenate(
                [filled[f, c, pl.ds(pl.multiple_of(in_column(q) * shots, shots), shots), :]
                 for c in range(2) for q in range(planes)], axis=0)
            dot = functools.partial(jnp.dot, preferred_element_type=jnp.float32)
            by_real, by_imag = dot(left, filled[f, 0]), dot(left, filled[f, 1])
            prod_real = by_real[:height] - by_imag[height:]
            prod_imag = by_imag[:height] + by_real[height:]
            which = (plane * tiles + t) * ROWS + f
            wave_real, wave_imag = wave_ref[0, which], wave_ref[1, which]
            out_real = -(wave_real * prod_real - wave_imag * prod_imag)
            out_imag = -(wave_real * prod_imag + wave_imag * prod_real)
            for q in range(points // LANES):
                lanes = slice(q * LANES, (q + 1) * LANES)
                ostage[0, q, pl.ds(f, height, stride=ROWS), :] = out_real[:, lanes]
                ostage[1, q, pl.ds(f, height, stride=ROWS), :] = out_imag[:, lanes]

        @pl.loop(0, planes)
        def _(z):
            rows = pl.ds(pl.multiple_of(z * shots * ROWS, shots * ROWS), shots * ROWS)
            for c in range(2):
                for q in range(points // LANES):
                    block = ostage[c, q, rows, :].reshape(shots, ROWS, LANES)
                    out[t, z, :, c, :, pl.ds(q * LANES, LANES)] = block.astype(jnp.bfloat16)

    def send_results(t):
        theirs = o_ref.at[:, :, plane * tiles + t]
        for q in range(planes):
            @pl.when(q != plane)
            def _(q=q):
                pltpu.make_async_remote_copy(out.at[t, q], theirs, out_send, out_recv,
                                             device_id={"shot": in_column(q)}, device_id_type=MESH).start()
        pltpu.make_async_copy(out.at[t, plane], theirs, own_in.at[t]).start()

    @pl.loop(0, tiles)
    def _(t):
        from_columns(t)
        sent = land.at[t, pl.ds(0, planes - 1)]
        pltpu.make_async_copy(sent, sent, column_out.at[t]).wait()
        pl.when((plane > 0) & (plane < planes - 1))(lambda: signal(go, in_column(outward)))

        @pl.when(held)
        def _():
            pl.semaphore_wait(go, 1)
            pl.when(t > 0)(lambda: send_results(t - 1))
            pl.when(t < tiles - 1)(lambda: send_all_traces(t + 1))

        from_chips(t)
        fill(t)
        multiply(t)
        pl.when((t == tiles - 1) | jnp.logical_not(held))(lambda: send_results(t))

    for t in range(tiles):
        pltpu.make_async_copy(out.at[t, 0], o_ref.at[:, :, t], own_in.at[t]).wait()
    shared = traces.at[:, :, :, pl.ds(0, (n - planes) * shots)]
    pltpu.make_async_copy(shared, shared, in_send).wait()
    others = o_ref.at[:, :, pl.ds(0, (planes - 1) * tiles)]
    pltpu.make_async_copy(others, others, out_send).wait()
    pltpu.make_async_copy(others, others, out_recv).wait()


def shards(n, spectra, fold_counts, inverse_wavelet):
    shots, _, bins, points = spectra.shape
    bf16, f32 = jnp.bfloat16, jnp.float32
    tiles = 2
    planes = bins // (tiles * ROWS)
    tiled = (shots, 2, bins // ROWS, ROWS, points)
    height = planes * shots
    landed = pl.pallas_call(
        functools.partial(kernel, planes, n),
        out_shape=pltpu.VMEM(tiled, bf16),
        in_specs=[pl.BlockSpec(memory_space=pl.ANY)] * 3,
        out_specs=pl.BlockSpec(memory_space=pltpu.VMEM),
        scratch_shapes=[
            pltpu.VMEM((tiles, planes, shots, 2, ROWS, points), bf16),
            pltpu.VMEM((2, points // LANES, shots * ROWS, LANES), f32),
            pltpu.VMEM((tiles, ROWS, 2, points, points), bf16),
            pltpu.VMEM((ROWS, 2, points, points), bf16),
            pltpu.VMEM((2, points // LANES, height * ROWS, LANES), f32),
            pltpu.VMEM((tiles, planes, shots, 2, ROWS, points), bf16),
            pltpu.VMEM((points, points), bf16),
            pltpu.VMEM((points, points), bf16),
            pltpu.VMEM((points, points), bf16),
            pltpu.VMEM((1, points), jnp.int32),
            pltpu.SMEM((2, bins), f32),
            pltpu.SemaphoreType.REGULAR((planes,)),
            pltpu.SemaphoreType.REGULAR,
            pltpu.SemaphoreType.REGULAR((n // planes // 2,)),
            pltpu.SemaphoreType.REGULAR,
            pltpu.VMEM((shots, 2, ROWS, points), bf16),
            pltpu.SemaphoreType.DMA,
            pltpu.SemaphoreType.DMA,
            pltpu.SemaphoreType.DMA((tiles,)),
            pltpu.SemaphoreType.DMA,
            pltpu.SemaphoreType.DMA((tiles,)),
            pltpu.SemaphoreType.DMA((tiles, planes)),
            pltpu.SemaphoreType.DMA((tiles,)),
            pltpu.SemaphoreType.DMA((tiles,)),
            pltpu.SemaphoreType.DMA,
            pltpu.SemaphoreType.DMA,
        ],
        compiler_params=pltpu.CompilerParams(
            collective_id=0, has_side_effects=True, vmem_limit_bytes=VMEM_BYTES),
    )(spectra.reshape(tiled), fold_counts[None, :], inverse_wavelet)
    return landed.reshape(spectra.shape)


def solution(mesh):
    spec = P(("groups", "shot"), None, None, None)
    return jax.shard_map(functools.partial(shards, mesh.shape["shot"]), mesh=mesh,
                         in_specs=(spec, P("groups"), P()), out_specs=spec, check_vma=False)
```

```python
import functools

import jax
import jax.numpy as jnp
from jax import lax
from jax.experimental import pallas as pl
from jax.experimental.pallas import tpu as pltpu
from jax.sharding import PartitionSpec as P

MESH = pl.DeviceIdType.MESH
VMEM_BYTES = 50 * 1024 * 1024
ROWS = 8
LANES = 128


def turn(eye, block):
    return lax.dot_general(eye, block, (((1,), (1,)), ((), ())),
                           preferred_element_type=jnp.float32).astype(jnp.bfloat16)


def kernel(planes, n, x_ref, row_hbm, wave_hbm, o_ref,
           land, stage, traces, filled, ostage, out, keep, swap, eye, row_ref, wave_ref,
           near_column, near_core, near_chip, go,
           first, first_in, small_in, own_in, in_send, column_out, column_in, chip_in, core_in, out_send, out_recv):
    shots, _, _, _, points = x_ref.shape
    tiles = land.shape[0]
    group = n // planes
    chips = group // 2
    me = lax.axis_index("shot")
    plane, place = me // group, lax.rem(me, group)
    chip, core = place // 2, lax.rem(place, 2)
    sibling = me + 1 - 2 * core

    def in_column(q):
        return q * group + place

    def in_plane(k):
        return plane * group + 2 * k + core

    def signal(sem, to):
        pl.semaphore_signal(sem, inc=1, device_id={"shot": to}, device_id_type=MESH)

    above = jnp.minimum(plane + 1, planes - 1)
    ready = pltpu.make_async_copy(x_ref.at[:, :, above * tiles], first, first_in)
    ready.start()

    barrier = pltpu.get_barrier_semaphore()
    for q in range(planes):
        pl.when(q > plane)(lambda q=q: signal(barrier, in_column(q)))
    pl.when(core == 1)(lambda: signal(barrier, sibling))
    for k in range(chips):
        pl.when(k > chip)(lambda k=k: signal(barrier, in_plane(k)))
    lower = plane + 1 - core + chip
    pl.when(lower > 0)(lambda: pl.semaphore_wait(barrier, lower))
    for q in range(planes):
        pl.when(q < plane)(lambda q=q: signal(near_column.at[plane], in_column(q)))
    pl.when(core == 0)(lambda: signal(near_core, sibling))
    for k in range(chips):
        pl.when(k < chip)(lambda k=k: signal(near_chip.at[chip], in_plane(k)))

    def rows_of(source):
        return pl.ds(pl.multiple_of(source * shots, shots), shots)

    def send(src, dst, sem, to):
        pltpu.make_async_remote_copy(src, dst, in_send, sem, device_id={"shot": to}, device_id_type=MESH).start()

    held = (plane < planes // 2 - 1) | (plane > planes // 2)
    outward = jnp.where(plane < planes // 2, plane - 1, plane + 1)

    def own(q, t):
        return x_ref.at[:, :, q * tiles + t]

    def send_traces(q, t):
        pltpu.make_async_remote_copy(own(q, t), land.at[t, plane], column_out.at[t], column_in.at[t, plane],
                                     device_id={"shot": in_column(q)}, device_id_type=MESH).start()

    def send_all_traces(t):
        for q in range(planes):
            pl.when(q != plane)(lambda q=q: send_traces(q, t))

    for q in range(planes):
        pl.when(q < plane)(lambda q=q: send_traces(q, 0))
    ready.wait()
    for q in range(planes):
        @pl.when(q > plane)
        def _(q=q):
            pl.semaphore_wait(near_column.at[q], 1)
            @pl.when(q == plane + 1)
            def _():
                pltpu.make_async_remote_copy(first, land.at[0, plane], column_out.at[0], column_in.at[0, plane],
                                             device_id={"shot": in_column(q)}, device_id_type=MESH).start()
            pl.when(q != plane + 1)(lambda: send_traces(q, 0))

    @pl.when(jnp.logical_not(held))
    def _():
        for t in range(1, tiles):
            send_all_traces(t)

    for t in range(tiles):
        pltpu.make_async_copy(own(plane, t), land.at[t, plane], own_in.at[t]).start()
    small = [pltpu.make_async_copy(row_hbm, row_ref, first_in), pltpu.make_async_copy(wave_hbm, wave_ref, small_in)]
    for copy in small:
        copy.start()

    def share(t, q):
        for c in range(2):
            flat = land[t, q, :, c].astype(jnp.float32).reshape(shots * ROWS, points)
            for k in range(points // LANES):
                stage[c, k] = flat[:, k * LANES : (k + 1) * LANES]
        mine = rows_of(in_column(q))
        for c in range(2):
            for f in range(ROWS):
                for k in range(points // LANES):
                    traces[t, f, c, mine, pl.ds(k * LANES, LANES)] = (
                        stage[c, k, pl.ds(f, shots, stride=ROWS), :].astype(jnp.bfloat16))
        piece = traces.at[t, :, :, mine]
        for k in range(chips):
            pl.when(k != chip)(lambda k=k: send(piece, piece, chip_in.at[t], in_plane(k)))
        send(piece, piece, core_in.at[t], sibling)

    pl.when(core == 1)(lambda: pl.semaphore_wait(near_core, 1))
    for k in range(chips):
        pl.when(k > chip)(lambda k=k: pl.semaphore_wait(near_chip.at[k], 1))

    @pl.loop(0, tiles)
    def _(t):
        pltpu.make_async_copy(land.at[t, plane], land.at[t, plane], own_in.at[t]).wait()
        share(t, plane)

    for copy in small:
        copy.wait()
    shot = lax.broadcasted_iota(jnp.int32, (points, points), 0)
    point = lax.broadcasted_iota(jnp.int32, (points, points), 1)
    eye[...] = jnp.where(shot == point, 1.0, 0.0).astype(jnp.bfloat16)
    mirrored = jnp.where(jnp.abs(shot - point) < row_ref[...], 1.0, 0.0).astype(jnp.bfloat16)
    keep[...] = turn(eye[...], mirrored)
    swap[...] = keep[...] * (1.0 - mirrored)

    def nearest_first(work):
        @pl.loop(1, planes)
        def _(d):
            pl.when(plane - d >= 0)(lambda: work(plane - d))
            pl.when(plane + d < planes)(lambda: work(plane + d))

    def from_columns(t):
        def one(q):
            pltpu.make_async_copy(land.at[t, q], land.at[t, q], column_in.at[t, q]).wait()
            share(t, q)

        nearest_first(one)

    def from_chips(t):
        if chips > 1:
            came = traces.at[t, :, :, pl.ds(0, planes * (chips - 1) * shots)]
            pltpu.make_async_copy(came, came, chip_in.at[t]).wait()

            @pl.loop(0, planes)
            def _(q):
                for k in range(chips):
                    @pl.when(k != chip)
                    def _(k=k):
                        piece = traces.at[t, :, :, rows_of(q * group + 2 * k + core)]
                        send(piece, piece, core_in.at[t], sibling)

        half = traces.at[t, :, :, pl.ds(0, n // 2 * shots)]
        pltpu.make_async_copy(half, half, core_in.at[t]).wait()

    def fill(t):
        @pl.loop(0, ROWS)
        def _(f):
            for c in range(2):
                block = traces[t, f, c]
                filled[f, c] = block * keep[...] + turn(eye[...], block * swap[...])

    def multiply(t):
        height = planes * shots

        @pl.loop(0, ROWS)
        def _(f):
            left = jnp.concatenate(
                [filled[f, c, pl.ds(pl.multiple_of(in_column(q) * shots, shots), shots), :]
                 for c in range(2) for q in range(planes)], axis=0)
            dot = functools.partial(jnp.dot, preferred_element_type=jnp.float32)
            by_real, by_imag = dot(left, filled[f, 0]), dot(left, filled[f, 1])
            prod_real = by_real[:height] - by_imag[height:]
            prod_imag = by_imag[:height] + by_real[height:]
            which = (plane * tiles + t) * ROWS + f
            wave_real, wave_imag = wave_ref[0, which], wave_ref[1, which]
            out_real = -(wave_real * prod_real - wave_imag * prod_imag)
            out_imag = -(wave_real * prod_imag + wave_imag * prod_real)
            for q in range(points // LANES):
                lanes = slice(q * LANES, (q + 1) * LANES)
                ostage[0, q, pl.ds(f, height, stride=ROWS), :] = out_real[:, lanes]
                ostage[1, q, pl.ds(f, height, stride=ROWS), :] = out_imag[:, lanes]

        @pl.loop(0, planes)
        def _(z):
            rows = pl.ds(pl.multiple_of(z * shots * ROWS, shots * ROWS), shots * ROWS)
            for c in range(2):
                for q in range(points // LANES):
                    block = ostage[c, q, rows, :].reshape(shots, ROWS, LANES)
                    out[t, z, :, c, :, pl.ds(q * LANES, LANES)] = block.astype(jnp.bfloat16)

    def send_results(t):
        theirs = o_ref.at[:, :, plane * tiles + t]
        def one(q):
            pltpu.make_async_remote_copy(out.at[t, q], theirs, out_send, out_recv,
                                         device_id={"shot": in_column(q)}, device_id_type=MESH).start()

        for d in reversed(range(1, planes)):
            pl.when(plane - d >= 0)(lambda: one(plane - d))
            pl.when(plane + d < planes)(lambda: one(plane + d))

        pltpu.make_async_copy(out.at[t, plane], theirs, own_in.at[t]).start()

    @pl.loop(0, tiles)
    def _(t):
        from_columns(t)
        sent = land.at[t, pl.ds(0, planes - 1)]
        pltpu.make_async_copy(sent, sent, column_out.at[t]).wait()
        pl.when((plane > 0) & (plane < planes - 1))(lambda: signal(go, in_column(outward)))

        @pl.when(held)
        def _():
            pl.semaphore_wait(go, 1)
            pl.when(t > 0)(lambda: send_results(t - 1))
            pl.when(t < tiles - 1)(lambda: send_all_traces(t + 1))

        from_chips(t)
        fill(t)
        multiply(t)
        pl.when((t == tiles - 1) | jnp.logical_not(held))(lambda: send_results(t))

    for t in range(tiles):
        pltpu.make_async_copy(out.at[t, 0], o_ref.at[:, :, t], own_in.at[t]).wait()
    shared = traces.at[:, :, :, pl.ds(0, (n - planes) * shots)]
    pltpu.make_async_copy(shared, shared, in_send).wait()
    others = o_ref.at[:, :, pl.ds(0, (planes - 1) * tiles)]
    pltpu.make_async_copy(others, others, out_send).wait()
    pltpu.make_async_copy(others, others, out_recv).wait()


def shards(n, spectra, fold_counts, inverse_wavelet):
    shots, _, bins, points = spectra.shape
    bf16, f32 = jnp.bfloat16, jnp.float32
    tiles = 2
    planes = bins // (tiles * ROWS)
    tiled = (shots, 2, bins // ROWS, ROWS, points)
    height = planes * shots
    landed = pl.pallas_call(
        functools.partial(kernel, planes, n),
        out_shape=pltpu.VMEM(tiled, bf16),
        in_specs=[pl.BlockSpec(memory_space=pl.ANY)] * 3,
        out_specs=pl.BlockSpec(memory_space=pltpu.VMEM),
        scratch_shapes=[
            pltpu.VMEM((tiles, planes, shots, 2, ROWS, points), bf16),
            pltpu.VMEM((2, points // LANES, shots * ROWS, LANES), f32),
            pltpu.VMEM((tiles, ROWS, 2, points, points), bf16),
            pltpu.VMEM((ROWS, 2, points, points), bf16),
            pltpu.VMEM((2, points // LANES, height * ROWS, LANES), f32),
            pltpu.VMEM((tiles, planes, shots, 2, ROWS, points), bf16),
            pltpu.VMEM((points, points), bf16),
            pltpu.VMEM((points, points), bf16),
            pltpu.VMEM((points, points), bf16),
            pltpu.VMEM((1, points), jnp.int32),
            pltpu.SMEM((2, bins), f32),
            pltpu.SemaphoreType.REGULAR((planes,)),
            pltpu.SemaphoreType.REGULAR,
            pltpu.SemaphoreType.REGULAR((n // planes // 2,)),
            pltpu.SemaphoreType.REGULAR,
            pltpu.VMEM((shots, 2, ROWS, points), bf16),
            pltpu.SemaphoreType.DMA,
            pltpu.SemaphoreType.DMA,
            pltpu.SemaphoreType.DMA((tiles,)),
            pltpu.SemaphoreType.DMA,
            pltpu.SemaphoreType.DMA((tiles,)),
            pltpu.SemaphoreType.DMA((tiles, planes)),
            pltpu.SemaphoreType.DMA((tiles,)),
            pltpu.SemaphoreType.DMA((tiles,)),
            pltpu.SemaphoreType.DMA,
            pltpu.SemaphoreType.DMA,
        ],
        compiler_params=pltpu.CompilerParams(
            collective_id=0, has_side_effects=True, vmem_limit_bytes=VMEM_BYTES),
    )(spectra.reshape(tiled), fold_counts[None, :], inverse_wavelet)
    return landed.reshape(spectra.shape)


def solution(mesh):
    spec = P(("groups", "shot"), None, None, None)
    return jax.shard_map(functools.partial(shards, mesh.shape["shot"]), mesh=mesh,
                         in_specs=(spec, P("groups"), P()), out_specs=spec, check_vma=False)
```

```python
import functools

import jax
import jax.numpy as jnp
from jax import lax
from jax.experimental import pallas as pl
from jax.experimental.pallas import tpu as pltpu
from jax.sharding import PartitionSpec as P

MESH = pl.DeviceIdType.MESH
VMEM_BYTES = 50 * 1024 * 1024
ROWS = 8
LANES = 128


def turn(eye, block):
    return lax.dot_general(eye, block, (((1,), (1,)), ((), ())),
                           preferred_element_type=jnp.float32).astype(jnp.bfloat16)


def kernel(planes, n, x_ref, row_hbm, wave_hbm, o_ref,
           land, stage, traces, filled, ostage, out, keep, swap, eye, row_ref, wave_ref,
           near_column, near_core, near_chip, go,
           first, first_in, small_in, own_in, in_send, column_out, column_in, chip_in, core_in, out_send, out_recv):
    shots, _, _, _, points = x_ref.shape
    tiles = land.shape[0]
    group = n // planes
    chips = group // 2
    me = lax.axis_index("shot")
    plane, place = me // group, lax.rem(me, group)
    chip, core = place // 2, lax.rem(place, 2)
    sibling = me + 1 - 2 * core

    def in_column(q):
        return q * group + place

    def in_plane(k):
        return plane * group + 2 * k + core

    def signal(sem, to):
        pl.semaphore_signal(sem, inc=1, device_id={"shot": to}, device_id_type=MESH)

    above = jnp.minimum(plane + 1, planes - 1)
    ready = pltpu.make_async_copy(x_ref.at[:, :, above * tiles], first, first_in)
    ready.start()

    under, over = plane == planes // 2 - 1, plane == planes // 2
    barrier = pltpu.get_barrier_semaphore()
    pl.when(over)(lambda: signal(barrier, in_column(plane - 1)))
    for q in range(planes):
        pl.when(q > plane)(lambda q=q: signal(barrier, in_column(q)))
    pl.when(core == 1)(lambda: signal(barrier, sibling))
    for k in range(chips):
        pl.when(k > chip)(lambda k=k: signal(barrier, in_plane(k)))
    lower = plane + 1 - core + chip + jnp.where(under, 1, 0)
    pl.when(lower > 0)(lambda: pl.semaphore_wait(barrier, lower))

    def send_first():
        pltpu.make_async_remote_copy(first, land.at[0, plane], column_out.at[0], column_in.at[0, plane],
                                     device_id={"shot": in_column(plane + 1)}, device_id_type=MESH).start()

    @pl.when(under)
    def _():
        ready.wait()
        send_first()

    for q in range(planes):
        pl.when((q < plane) & jnp.logical_not(over & (q == plane - 1)))(
            lambda q=q: signal(near_column.at[plane], in_column(q)))
    pl.when(core == 0)(lambda: signal(near_core, sibling))
    for k in range(chips):
        pl.when(k < chip)(lambda k=k: signal(near_chip.at[chip], in_plane(k)))

    def rows_of(source):
        return pl.ds(pl.multiple_of(source * shots, shots), shots)

    def send(src, dst, sem, to):
        pltpu.make_async_remote_copy(src, dst, in_send, sem, device_id={"shot": to}, device_id_type=MESH).start()

    held = (plane < planes // 2 - 1) | (plane > planes // 2)
    outward = jnp.where(plane < planes // 2, plane - 1, plane + 1)

    def own(q, t):
        return x_ref.at[:, :, q * tiles + t]

    def send_traces(q, t):
        pltpu.make_async_remote_copy(own(q, t), land.at[t, plane], column_out.at[t], column_in.at[t, plane],
                                     device_id={"shot": in_column(q)}, device_id_type=MESH).start()

    def send_all_traces(t):
        for q in range(planes):
            pl.when(q != plane)(lambda q=q: send_traces(q, t))

    for q in range(planes):
        pl.when(q < plane)(lambda q=q: send_traces(q, 0))
    @pl.when(jnp.logical_not(under))
    def _():
        ready.wait()
        for q in range(planes):
            @pl.when(q > plane)
            def _(q=q):
                pl.semaphore_wait(near_column.at[q], 1)
                pl.when(q == plane + 1)(lambda: send_first())
                pl.when(q != plane + 1)(lambda: send_traces(q, 0))

    @pl.when(under)
    def _():
        for q in range(planes):
            @pl.when(q > plane + 1)
            def _(q=q):
                pl.semaphore_wait(near_column.at[q], 1)
                send_traces(q, 0)

    @pl.when(jnp.logical_not(held))
    def _():
        for t in range(1, tiles):
            send_all_traces(t)

    for t in range(tiles):
        pltpu.make_async_copy(own(plane, t), land.at[t, plane], own_in.at[t]).start()
    small = [pltpu.make_async_copy(row_hbm, row_ref, first_in), pltpu.make_async_copy(wave_hbm, wave_ref, small_in)]
    for copy in small:
        copy.start()

    def share(t, q):
        for c in range(2):
            flat = land[t, q, :, c].astype(jnp.float32).reshape(shots * ROWS, points)
            for k in range(points // LANES):
                stage[c, k] = flat[:, k * LANES : (k + 1) * LANES]
        mine = rows_of(in_column(q))
        for c in range(2):
            for f in range(ROWS):
                for k in range(points // LANES):
                    traces[t, f, c, mine, pl.ds(k * LANES, LANES)] = (
                        stage[c, k, pl.ds(f, shots, stride=ROWS), :].astype(jnp.bfloat16))
        piece = traces.at[t, :, :, mine]
        for k in range(chips):
            pl.when(k != chip)(lambda k=k: send(piece, piece, chip_in.at[t], in_plane(k)))
        send(piece, piece, core_in.at[t], sibling)

    pl.when(core == 1)(lambda: pl.semaphore_wait(near_core, 1))
    for k in range(chips):
        pl.when(k > chip)(lambda k=k: pl.semaphore_wait(near_chip.at[k], 1))

    @pl.loop(0, tiles)
    def _(t):
        pltpu.make_async_copy(land.at[t, plane], land.at[t, plane], own_in.at[t]).wait()
        share(t, plane)

    for copy in small:
        copy.wait()
    shot = lax.broadcasted_iota(jnp.int32, (points, points), 0)
    point = lax.broadcasted_iota(jnp.int32, (points, points), 1)
    eye[...] = jnp.where(shot == point, 1.0, 0.0).astype(jnp.bfloat16)
    mirrored = jnp.where(jnp.abs(shot - point) < row_ref[...], 1.0, 0.0).astype(jnp.bfloat16)
    keep[...] = turn(eye[...], mirrored)
    swap[...] = keep[...] * (1.0 - mirrored)

    def nearest_first(work):
        @pl.loop(1, planes)
        def _(d):
            pl.when(plane - d >= 0)(lambda: work(plane - d))
            pl.when(plane + d < planes)(lambda: work(plane + d))

    def from_columns(t):
        def one(q):
            pltpu.make_async_copy(land.at[t, q], land.at[t, q], column_in.at[t, q]).wait()
            share(t, q)

        nearest_first(one)

    def from_chips(t):
        if chips > 1:
            came = traces.at[t, :, :, pl.ds(0, planes * (chips - 1) * shots)]
            pltpu.make_async_copy(came, came, chip_in.at[t]).wait()

            @pl.loop(0, planes)
            def _(q):
                for k in range(chips):
                    @pl.when(k != chip)
                    def _(k=k):
                        piece = traces.at[t, :, :, rows_of(q * group + 2 * k + core)]
                        send(piece, piece, core_in.at[t], sibling)

        half = traces.at[t, :, :, pl.ds(0, n // 2 * shots)]
        pltpu.make_async_copy(half, half, core_in.at[t]).wait()

    def fill(t):
        @pl.loop(0, ROWS)
        def _(f):
            for c in range(2):
                block = traces[t, f, c]
                filled[f, c] = block * keep[...] + turn(eye[...], block * swap[...])

    def multiply(t):
        height = planes * shots

        @pl.loop(0, ROWS)
        def _(f):
            left = jnp.concatenate(
                [filled[f, c, pl.ds(pl.multiple_of(in_column(q) * shots, shots), shots), :]
                 for c in range(2) for q in range(planes)], axis=0)
            dot = functools.partial(jnp.dot, preferred_element_type=jnp.float32)
            by_real, by_imag = dot(left, filled[f, 0]), dot(left, filled[f, 1])
            prod_real = by_real[:height] - by_imag[height:]
            prod_imag = by_imag[:height] + by_real[height:]
            which = (plane * tiles + t) * ROWS + f
            wave_real, wave_imag = wave_ref[0, which], wave_ref[1, which]
            out_real = -(wave_real * prod_real - wave_imag * prod_imag)
            out_imag = -(wave_real * prod_imag + wave_imag * prod_real)
            for q in range(points // LANES):
                lanes = slice(q * LANES, (q + 1) * LANES)
                ostage[0, q, pl.ds(f, height, stride=ROWS), :] = out_real[:, lanes]
                ostage[1, q, pl.ds(f, height, stride=ROWS), :] = out_imag[:, lanes]

        @pl.loop(0, planes)
        def _(z):
            rows = pl.ds(pl.multiple_of(z * shots * ROWS, shots * ROWS), shots * ROWS)
            for c in range(2):
                for q in range(points // LANES):
                    block = ostage[c, q, rows, :].reshape(shots, ROWS, LANES)
                    out[t, z, :, c, :, pl.ds(q * LANES, LANES)] = block.astype(jnp.bfloat16)

    def send_results(t):
        theirs = o_ref.at[:, :, plane * tiles + t]
        for q in range(planes):
            @pl.when(q != plane)
            def _(q=q):
                pltpu.make_async_remote_copy(out.at[t, q], theirs, out_send, out_recv,
                                             device_id={"shot": in_column(q)}, device_id_type=MESH).start()
        pltpu.make_async_copy(out.at[t, plane], theirs, own_in.at[t]).start()

    @pl.loop(0, tiles)
    def _(t):
        from_columns(t)
        sent = land.at[t, pl.ds(0, planes - 1)]
        pltpu.make_async_copy(sent, sent, column_out.at[t]).wait()
        pl.when((plane > 0) & (plane < planes - 1))(lambda: signal(go, in_column(outward)))

        @pl.when(held)
        def _():
            pl.semaphore_wait(go, 1)
            pl.when(t > 0)(lambda: send_results(t - 1))
            pl.when(t < tiles - 1)(lambda: send_all_traces(t + 1))

        from_chips(t)
        fill(t)
        multiply(t)
        pl.when((t == tiles - 1) | jnp.logical_not(held))(lambda: send_results(t))

    for t in range(tiles):
        pltpu.make_async_copy(out.at[t, 0], o_ref.at[:, :, t], own_in.at[t]).wait()
    shared = traces.at[:, :, :, pl.ds(0, (n - planes) * shots)]
    pltpu.make_async_copy(shared, shared, in_send).wait()
    others = o_ref.at[:, :, pl.ds(0, (planes - 1) * tiles)]
    pltpu.make_async_copy(others, others, out_send).wait()
    pltpu.make_async_copy(others, others, out_recv).wait()


def shards(n, spectra, fold_counts, inverse_wavelet):
    shots, _, bins, points = spectra.shape
    bf16, f32 = jnp.bfloat16, jnp.float32
    tiles = 2
    planes = bins // (tiles * ROWS)
    tiled = (shots, 2, bins // ROWS, ROWS, points)
    height = planes * shots
    landed = pl.pallas_call(
        functools.partial(kernel, planes, n),
        out_shape=pltpu.VMEM(tiled, bf16),
        in_specs=[pl.BlockSpec(memory_space=pl.ANY)] * 3,
        out_specs=pl.BlockSpec(memory_space=pltpu.VMEM),
        scratch_shapes=[
            pltpu.VMEM((tiles, planes, shots, 2, ROWS, points), bf16),
            pltpu.VMEM((2, points // LANES, shots * ROWS, LANES), f32),
            pltpu.VMEM((tiles, ROWS, 2, points, points), bf16),
            pltpu.VMEM((ROWS, 2, points, points), bf16),
            pltpu.VMEM((2, points // LANES, height * ROWS, LANES), f32),
            pltpu.VMEM((tiles, planes, shots, 2, ROWS, points), bf16),
            pltpu.VMEM((points, points), bf16),
            pltpu.VMEM((points, points), bf16),
            pltpu.VMEM((points, points), bf16),
            pltpu.VMEM((1, points), jnp.int32),
            pltpu.SMEM((2, bins), f32),
            pltpu.SemaphoreType.REGULAR((planes,)),
            pltpu.SemaphoreType.REGULAR,
            pltpu.SemaphoreType.REGULAR((n // planes // 2,)),
            pltpu.SemaphoreType.REGULAR,
            pltpu.VMEM((shots, 2, ROWS, points), bf16),
            pltpu.SemaphoreType.DMA,
            pltpu.SemaphoreType.DMA,
            pltpu.SemaphoreType.DMA((tiles,)),
            pltpu.SemaphoreType.DMA,
            pltpu.SemaphoreType.DMA((tiles,)),
            pltpu.SemaphoreType.DMA((tiles, planes)),
            pltpu.SemaphoreType.DMA((tiles,)),
            pltpu.SemaphoreType.DMA((tiles,)),
            pltpu.SemaphoreType.DMA,
            pltpu.SemaphoreType.DMA,
        ],
        compiler_params=pltpu.CompilerParams(
            collective_id=0, has_side_effects=True, vmem_limit_bytes=VMEM_BYTES),
    )(spectra.reshape(tiled), fold_counts[None, :], inverse_wavelet)
    return landed.reshape(spectra.shape)


def solution(mesh):
    spec = P(("groups", "shot"), None, None, None)
    return jax.shard_map(functools.partial(shards, mesh.shape["shot"]), mesh=mesh,
                         in_specs=(spec, P("groups"), P()), out_specs=spec, check_vma=False)
```
